256 devices in a mesh: stripe: 32 (over z, x_lo, core), tile: 8 (over y, x_hi).
Axes of the slice: x: 4 (x_hi: 2, x_lo: 2; x = x_hi * 2 + x_lo), y: 4, z: 8, core: 2. Of those that a mesh axis runs over, the one named last changes fastest.
Arguments:
- positions: int32 [32, 24], P('stripe', 'tile'), may hold values from -64 to -64, as said below
- row_offsets: int32 [32, 24], P('stripe', 'tile'), may hold values from -64 to 64, as said below
- amplitudes: float32 [32, 24, 256, 256], P('stripe', 'tile'), may hold values from 0 to 2
- object_field: float32 [2, 8192, 1024], P(None, 'stripe', 'tile'), may hold values from -6 to 6
- probe_field: float32 [2, 256, 256], replicated, may hold values from -6 to 6
Outputs:
- object_out: float32 [2, 8192, 1024], P(None, 'stripe', 'tile')
- probe_out: float32 [2, 256, 256], replicated
The draws below stay inside these ranges and needn't reach their ends.
Inputs may be any that keep to these rules, and one draw needn't show every extreme that they name: `positions`: in every block of 3 patterns of one stripe and one tile, the first offset is -64 and the second is 128 - 192. `row_offsets`: in every block of 3 patterns of one stripe and one tile, the first row offset is -64 and the second is 64.
All inputs are finite; a program needn't handle non-finite values.
Results may differ from the reference program's by a relative error of at most 0.0006.
The reference program's roundings to bfloat16 on the way count: a program that leaves them out, or rounds other values in their place, can miss the bound.
Values sent between devices are 32-bit elements; how exact they have to be, the bound alone decides.
No kernel may reach another device: no remote copies, remote signals or barrier semaphores. Data moves between devices by JAX's collectives and lax.ppermute only.
A program may use at most 64 MiB of HBM per device.

```python
import math
import jax
import jax.numpy as jnp
from jax import lax

PW = 256
HALO = 64
TILE_W = 128
PAT_DEV = 3
INNER = 2
OUTER = 2
STRIPES = 32
PATTERNS = 24
OH = 8192
OW = 1024


def draw_positions(key, part):
    lowest = -HALO
    highest = TILE_W + HALO - PW
    own_key = jax.random.fold_in(key, 3)
    values = jax.random.randint(own_key, (STRIPES, PATTERNS), lowest, highest + 1)
    within = jnp.arange(PATTERNS, dtype=jnp.int32) % PAT_DEV
    values = jnp.where(within[None, :] == 0, lowest, jnp.where(within[None, :] == 1, highest, values))
    return values.astype(jnp.int32)


def draw_row_offsets(key, part):
    own_key = jax.random.fold_in(key, 7)
    values = jax.random.randint(own_key, (STRIPES, PATTERNS), -HALO, HALO + 1)
    within = jnp.arange(PATTERNS, dtype=jnp.int32) % PAT_DEV
    values = jnp.where(within[None, :] == 0, -HALO, jnp.where(within[None, :] == 1, HALO, values))
    return values.astype(jnp.int32)


def levels(key, dims, pieces, low, high):
    def one(axis_at, shards_of):
        heights = jax.random.uniform(jax.random.fold_in(jax.random.fold_in(key, 6), axis_at), (shards_of,), jnp.float32, low / len(pieces), high / len(pieces))
        return jnp.repeat(jnp.exp(heights), dims[axis_at] // shards_of).reshape((-1,) + (1,) * (len(dims) - axis_at - 1))

    loudness = one(*pieces[0])
    for cut in pieces[1:]:
        loudness = loudness * one(*cut)
    return loudness


def noise(key, shape, width, most, split=(), kind=jnp.bfloat16):
    result = jax.random.normal(key, shape, jnp.float32) * width
    if len(split) > 0:
        result = levels(key, shape, split, -0.22, 0.18) * result
    return jnp.clip(result, min=-most, max=most).astype(kind)


def setup_inputs(seed: int = 0) -> dict:
    splits = jax.random.split(jax.random.key(seed), 6)
    positions = draw_positions(jax.random.fold_in(splits[5], 71), 0)
    row_offsets = draw_row_offsets(jax.random.fold_in(splits[5], 71), 0)
    amplitudes = jnp.clip(2.0 * jax.random.uniform(splits[2], (STRIPES, PATTERNS, PW, PW), jnp.float32) ** levels(splits[2], (STRIPES, PATTERNS, PW, PW), ((0, 32), (1, 8)), -0.2, 0.2), 0.0, 2.0)
    object_field = noise(splits[3], (2, OH, OW), 1.0, 6.0, ((1, 32), (2, 8)), jnp.float32)
    probe_field = noise(splits[4], (2, PW, PW), 1.0, 6.0, (), jnp.float32)
    return dict(positions=positions, row_offsets=row_offsets, amplitudes=amplitudes, object_field=object_field, probe_field=probe_field)


def dft_tables():
    indices = jnp.arange(PW, dtype=jnp.int32)
    phase = indices[:, None] * indices[None, :] % PW
    angles = phase.astype(jnp.float32) * (2.0 * math.pi / PW)
    factor = 1.0 / math.sqrt(PW)
    return ((jnp.cos(angles) * factor).astype(jnp.bfloat16), (jnp.sin(angles) * factor).astype(jnp.bfloat16))

def apply_left(matrix, batch):
    return jnp.einsum('kn,pnm->pkm', matrix.astype(jnp.float32), batch.astype(jnp.float32))

def apply_right(batch, matrix):
    return jnp.einsum('pkn,nm->pkm', batch.astype(jnp.float32), matrix.astype(jnp.float32))

def pattern_pass(windows, probe_field, measured, cosine, sine):
    win_re = windows[:, 0]
    win_im = windows[:, 1]
    probe_re = probe_field[0]
    probe_im = probe_field[1]
    exit_re = (probe_re * win_re - probe_im * win_im).astype(jnp.bfloat16)
    exit_im = (probe_re * win_im + probe_im * win_re).astype(jnp.bfloat16)
    half_re = (apply_left(cosine, exit_re) + apply_left(sine, exit_im)).astype(jnp.bfloat16)
    half_im = (apply_left(cosine, exit_im) - apply_left(sine, exit_re)).astype(jnp.bfloat16)
    spec_re = apply_right(half_re, cosine) + apply_right(half_im, sine)
    spec_im = apply_right(half_im, cosine) - apply_right(half_re, sine)
    magnitude = jnp.sqrt(spec_re * spec_re + spec_im * spec_im)
    scaling = measured / jnp.maximum(magnitude, 0.5)
    miss_re = (spec_re - scaling * spec_re).astype(jnp.bfloat16)
    miss_im = (spec_im - scaling * spec_im).astype(jnp.bfloat16)
    hb_re = (apply_left(cosine, miss_re) - apply_left(sine, miss_im)).astype(jnp.bfloat16)
    hb_im = (apply_left(cosine, miss_im) + apply_left(sine, miss_re)).astype(jnp.bfloat16)
    back_re = apply_right(hb_re, cosine) - apply_right(hb_im, sine)
    back_im = apply_right(hb_im, cosine) + apply_right(hb_re, sine)
    object_grad = jnp.stack([probe_re * back_re + probe_im * back_im, probe_re * back_im - probe_im * back_re], axis=1)
    probe_grad = jnp.stack([lax.optimization_barrier(jnp.sum(win_re * back_re + win_im * back_im, axis=0)), lax.optimization_barrier(jnp.sum(win_re * back_im - win_im * back_re, axis=0))])
    illumination = lax.optimization_barrier(jnp.sum(win_re * win_re + win_im * win_im, axis=0))
    return (object_grad, probe_grad, illumination)

def reference(positions, row_offsets, amplitudes, object_field, probe_field):
    cosine, sine = dft_tables()
    padded_width = OW + 2 * HALO
    padded_height = OH + 2 * HALO
    tile_start = jnp.arange(PATTERNS, dtype=jnp.int32) // PAT_DEV * TILE_W
    starts_all = (positions + tile_start[None, :] + HALO).astype(jnp.int32)
    stripe_top = jnp.arange(STRIPES, dtype=jnp.int32) * PW
    rows_all = (row_offsets + stripe_top[:, None] + HALO).astype(jnp.int32)
    zero_index = jnp.zeros((), jnp.int32)
    current = object_field
    for outer_step in range(OUTER):
        grad_sum = jnp.zeros((2, PW, PW), jnp.float32)
        light_sum = jnp.zeros((PW, PW), jnp.float32)
        for inner_step in range(INNER):
            padded = jnp.pad(current, ((0, 0), (HALO, HALO), (HALO, HALO)))
            step_size = 1.0 / (2.0 * PAT_DEV * jnp.max(probe_field[0] * probe_field[0] + probe_field[1] * probe_field[1]) + 1e-06)

            def stripe_pass(carry, stripe):
                starts = starts_all[stripe]
                row_list = rows_all[stripe]
                windows = jax.vmap(lambda row_start, column_start: lax.dynamic_slice(padded, (zero_index, row_start, column_start), (2, PW, PW)))(row_list, starts)
                object_grad, probe_grad, illumination = pattern_pass(windows, probe_field, amplitudes[stripe], cosine, sine)

                def add_one(pattern, total):
                    where = (zero_index, row_list[pattern], starts[pattern])
                    before = lax.dynamic_slice(total, where, (2, PW, PW))
                    return lax.dynamic_update_slice(total, before + object_grad[pattern], where)
                full_total = lax.fori_loop(0, PATTERNS, add_one, carry[2])
                return ((carry[0] + probe_grad, carry[1] + illumination, full_total), None)
            start_carry = (jnp.zeros((2, PW, PW), jnp.float32), jnp.zeros((PW, PW), jnp.float32), jnp.zeros((2, padded_height, padded_width), jnp.float32))
            (grad_sum, light_sum, full_grad), unused = lax.scan(stripe_pass, start_carry, jnp.arange(STRIPES, dtype=jnp.int32))
            current = current - step_size * full_grad[:, HALO:HALO + OH, HALO:HALO + OW]
        probe_field = probe_field - 0.5 * grad_sum / (light_sum + 1.0)
    return (current, probe_field)
```

```python
import functools
import math

import jax
import jax.numpy as jnp
from jax import lax
from jax.experimental import pallas as pl
from jax.experimental.pallas import tpu as pltpu
from jax.sharding import PartitionSpec as P

PW = 256
HALO = 64
TILE_W = 128
PAT_DEV = 3
STRIPES = 32
TILES = 8
EXT = PW + 2 * HALO
LANES = 128
AXES = ("stripe", "tile")
F32 = jnp.float32
BF16 = jnp.bfloat16


def place(x, y, z, core):
    return (z * 4 + (x % 2) * 2 + core) * TILES + y * 2 + x // 2


def physical(flat):
    s, t = flat // TILES, flat % TILES
    return (t % 2) * 2 + (s // 2) % 2, t // 2, s // 4, s % 2


def moved(step):
    pairs = []
    for flat in range(STRIPES * TILES):
        pairs.append((flat, place(*step(*physical(flat)))))
    return pairs


def core_swap():
    return moved(lambda x, y, z, c: (x, y, z, 1 - c))


def along_x(k):
    return moved(lambda x, y, z, c: ((x + k) % 4, y, z, c))


def along_y(k):
    return moved(lambda x, y, z, c: (x, (y + k) % 4, z, c))


def along_z(k):
    return moved(lambda x, y, z, c: (x, y, z ^ k, c))


def neighbour(ds, dt):
    pairs = []
    for s in range(STRIPES):
        for t in range(TILES):
            s2, t2 = s + ds, t + dt
            if 0 <= s2 < STRIPES and 0 <= t2 < TILES:
                pairs.append((s * TILES + t, s2 * TILES + t2))
    return pairs


def send(value, pairs):
    return lax.ppermute(value, AXES, pairs)


def dft_tables():
    indices = jnp.arange(PW, dtype=jnp.int32)
    phase = indices[:, None] * indices[None, :] % PW
    angles = phase.astype(jnp.float32) * (2.0 * math.pi / PW)
    factor = 1.0 / math.sqrt(PW)
    cosine = (jnp.cos(angles) * factor).astype(jnp.bfloat16)
    sine = (jnp.sin(angles) * factor).astype(jnp.bfloat16)
    forward = jnp.concatenate(
        [jnp.concatenate([cosine, sine], 1), jnp.concatenate([-sine, cosine], 1)], 0
    )
    inverse = jnp.concatenate(
        [jnp.concatenate([cosine, -sine], 1), jnp.concatenate([sine, cosine], 1)], 0
    )
    return forward, inverse


def vmem_call(kernel, name, out_shapes, scratch, *args):
    smem = pl.BlockSpec(memory_space=pltpu.SMEM)
    vmem = pl.BlockSpec(memory_space=pltpu.VMEM)
    return pl.pallas_call(
        kernel,
        name=name,
        in_specs=[smem if a.dtype == jnp.int32 else vmem for a in args],
        out_specs=[vmem for _ in out_shapes],
        out_shape=[jax.ShapeDtypeStruct(s, F32) for s in out_shapes],
        scratch_shapes=scratch,
    )(*args)


def step_of(probe_ref):
    power = probe_ref[0] * probe_ref[0] + probe_ref[1] * probe_ref[1]
    return 1.0 / (2.0 * PAT_DEV * jnp.max(power) + 1e-06)


def updated(place_ref, probe_ref, obj_ref, parts, store, rows, lanes):
    gl, gr, rl, rr, rt, rb = parts
    step = step_of(probe_ref)
    s, t = place_ref[1], place_ref[2]
    row_lo = jnp.where(s == 0, HALO, 0)
    row_hi = jnp.where(s == STRIPES - 1, HALO + PW, EXT)
    col_lo = jnp.where(t == 0, HALO, 0)
    col_hi = jnp.where(t == TILES - 1, HALO + TILE_W, PW)
    for side, own, other in ((0, gl, rl), (1, gr, rr)):
        cols = slice(side * LANES, (side + 1) * LANES)
        row = lax.broadcasted_iota(jnp.int32, (LANES, LANES), 0)
        col = lax.broadcasted_iota(jnp.int32, (LANES, LANES), 1) + side * LANES
        col_ok = (col >= col_lo) & (col < col_hi)
        for block in range(3):
            span = slice(block * LANES, (block + 1) * LANES)
            at = row + block * LANES
            ok = col_ok & (at >= row_lo) & (at < row_hi)
            factor = jnp.where(ok, step, 0.0)
            for ch in range(2):
                g = own[ch, span, :] + other[ch, span, :]
                if block == 0:
                    g = g + rt[ch, :, cols]
                if block == 2:
                    g = g + rb[ch, :, cols]
                store(ch, block, side, obj_ref[ch, span, cols] - factor * g)


def new_probe(place_ref, probe_ref, near_ref, far_ref, total_ref, out_ref):
    c, x, y = place_ref[3], place_ref[4], place_ref[5]
    for k in range(4):
        for j in range(4):
            block = ((x + 4 - k) % 4) * 4 + (y + 4 - j) % 4
            for half, ref in ((c, near_ref), (1 - c, far_ref)):
                row = pl.multiple_of((half * 16 + block) * 8, 8)
                for ch in range(3):
                    total_ref[ch, pl.ds(row, 8), :] = ref[k * 4 + j, ch * 8 : ch * 8 + 8, :]
    scale = 0.5 / (total_ref[2] + 1.0)
    for ch in range(2):
        out_ref[ch] = probe_ref[ch] - total_ref[ch] * scale


def lifted(value, shift):
    tiles = value.reshape(PW // 8 + 1, 8, value.shape[1])
    tiles = pltpu.roll(tiles, (8 - shift) % 8, axis=1)
    row = lax.broadcasted_iota(jnp.int32, (PW // 8, 8, value.shape[1]), 1)
    return jnp.where(row < 8 - shift, tiles[:-1], tiles[1:]).reshape(PW, value.shape[1])


def lowered(value, shift):
    tiles = value.reshape(PW // 8, 8, value.shape[1])
    tiles = pltpu.roll(tiles, shift % 8, axis=1)
    none = jnp.zeros((1, 8, value.shape[1]), F32)
    row = lax.broadcasted_iota(jnp.int32, (PW // 8 + 1, 8, value.shape[1]), 1)
    below = jnp.concatenate([tiles, none], axis=0)
    above = jnp.concatenate([none, tiles], axis=0)
    return jnp.where(row >= shift, below, above).reshape(PW + 8, value.shape[1])


def patterns(place_ref, obj_ref, probe_ref, amp_ref, fwd_ref, inv_ref, gl_ref, gr_ref, pg_ref):
    fwd, inv = fwd_ref[...], inv_ref[...]
    third, shift = pl.multiple_of(place_ref[0], 8), place_ref[6]
    for p in range(PAT_DEV):
        if p < 2:
            rows = pl.ds((0, 2 * HALO)[p], PW)
            wr, wi = obj_ref[0, rows, :], obj_ref[1, rows, :]
        else:
            wr, wi = [lifted(obj_ref[ch, pl.ds(third, PW + 8), :], shift) for ch in range(2)]
        pr, pi = probe_ref[0], probe_ref[1]
        exit_wave = jnp.concatenate(
            [(pr * wr - pi * wi).astype(BF16), (pr * wi + pi * wr).astype(BF16)], axis=0
        )
        half = jnp.dot(fwd, exit_wave, preferred_element_type=F32)
        half = jnp.concatenate([half[:PW].astype(BF16), half[PW:].astype(BF16)], axis=1)
        spec = jnp.dot(half, inv, preferred_element_type=F32)
        sr, si = spec[:, :PW], spec[:, PW:]
        scaling = amp_ref[p] * lax.rsqrt(jnp.maximum(sr * sr + si * si, 0.25))
        miss = jnp.concatenate(
            [(sr - scaling * sr).astype(BF16), (si - scaling * si).astype(BF16)], axis=0
        )
        half = jnp.dot(inv, miss, preferred_element_type=F32)
        half = jnp.concatenate([half[:PW].astype(BF16), half[PW:].astype(BF16)], axis=1)
        back = jnp.dot(half, fwd, preferred_element_type=F32)
        br, bi = back[:, :PW], back[:, PW:]
        for ch, og in ((0, pr * br + pi * bi), (1, pr * bi - pi * br)):
            for ref, part in ((gl_ref, og[:, :LANES]), (gr_ref, og[:, LANES:])):
                if p == 0:
                    ref[ch, 0:PW, :] = part
                elif p == 1:
                    ref[ch, 2 * HALO : PW, :] += part[: 2 * HALO]
                    ref[ch, PW:EXT, :] = part[2 * HALO :]
                else:
                    ref[ch, pl.ds(third, PW + 8), :] += lowered(part, shift)
        if pg_ref is not None:
            sums = (wr * br + wi * bi, wr * bi - wi * br, wr * wr + wi * wi)
            for ch, value in enumerate(sums):
                if p == 0:
                    pg_ref[ch] = value
                else:
                    pg_ref[ch] += value


def split_probe_grad(place_ref, pg_ref, keep_ref, send_ref):
    c, x, y = place_ref[3], place_ref[4], place_ref[5]
    for k in range(4):
        for j in range(4):
            block = ((x + k) % 4) * 4 + (y + j) % 4
            for half, ref in ((c, keep_ref), (1 - c, send_ref)):
                row = pl.multiple_of((half * 16 + block) * 8, 8)
                for ch in range(3):
                    ref[k * 4 + j, ch * 8 : ch * 8 + 8, :] = pg_ref[ch, pl.ds(row, 8), :]


def pass_kernel(first, last_inner, fresh_probe, *refs):
    refs = list(refs)
    place_ref = refs.pop(0)
    obj_ref = refs.pop(0)
    parts = None if first else [refs.pop(0) for _ in range(6)]
    probe_ref = refs.pop(0)
    sums = [refs.pop(0) for _ in range(2)] if fresh_probe else None
    amp_ref, fwd_ref, inv_ref = [refs.pop(0) for _ in range(3)]
    gl_ref, gr_ref = [refs.pop(0) for _ in range(2)]
    if not first:
        out_ref = refs.pop(0)

        def store(ch, block, side, value):
            rows = slice(block * LANES, (block + 1) * LANES)
            out_ref[ch, rows, side * LANES : (side + 1) * LANES] = value

        updated(place_ref, probe_ref, obj_ref, parts, store, None, None)
        obj_ref = out_ref
    if fresh_probe:
        fresh_ref = refs.pop(0)
    if last_inner:
        keep_ref, send_ref = [refs.pop(0) for _ in range(2)]
    if fresh_probe:
        new_probe(place_ref, probe_ref, sums[0], sums[1], refs[-1], fresh_ref)
        probe_ref = fresh_ref
    pg_ref = refs[-1] if last_inner else None
    patterns(place_ref, obj_ref, probe_ref, amp_ref, fwd_ref, inv_ref, gl_ref, gr_ref, pg_ref)
    if last_inner:
        split_probe_grad(place_ref, pg_ref, keep_ref, send_ref)


def run_pass(where, obj, parts, probe, sums, amp, tables, last_inner):
    first, fresh = parts is None, sums is not None
    args = [where, obj] + ([] if first else list(parts)) + [probe]
    args += (list(sums) if fresh else []) + [amp, *tables]
    outs = [(2, EXT, LANES)] * 2
    outs += [] if first else [(2, EXT, PW)]
    outs += [(2, PW, PW)] if fresh else []
    outs += [(16, 24, PW)] * 2 if last_inner else []
    scratch = [pltpu.VMEM((3, PW, PW), F32)] if fresh or last_inner else []
    kernel = functools.partial(pass_kernel, first, last_inner, fresh)
    got = list(vmem_call(kernel, "object_pass", outs, scratch, *args))
    gl, gr = got.pop(0), got.pop(0)
    obj = obj if first else got.pop(0)
    probe = got.pop(0) if fresh else probe
    return gl, gr, obj, probe, got


def object_kernel(place_ref, obj_ref, gl, gr, rl, rr, rt, rb, probe_ref, out_ref, tmp_ref):
    def store(ch, block, side, value):
        rows = slice(block * LANES, (block + 1) * LANES)
        tmp_ref[ch, rows, side * LANES : (side + 1) * LANES] = value

    updated(place_ref, probe_ref, obj_ref, (gl, gr, rl, rr, rt, rb), store, None, None)
    out_ref[...] = tmp_ref[:, HALO : HALO + PW, HALO : HALO + TILE_W]


def probe_kernel(place_ref, probe_ref, near_ref, far_ref, out_ref, total_ref):
    new_probe(place_ref, probe_ref, near_ref, far_ref, total_ref, out_ref)


def exchange(gl, gr):
    rl = send(gr, neighbour(0, 1))
    rr = send(gl, neighbour(0, -1))

    def edges(gl, gr, rl, rr, top, bottom):
        for ch in range(2):
            for cols, a, b in ((slice(0, LANES), gl, rl), (slice(LANES, PW), gr, rr)):
                top[ch, :, cols] = a[ch, 0:LANES, :] + b[ch, 0:LANES, :]
                bottom[ch, :, cols] = a[ch, PW:EXT, :] + b[ch, PW:EXT, :]

    top, bottom = vmem_call(edges, "edges", [(2, LANES, PW)] * 2, [], gl, gr, rl, rr)
    rt = send(bottom, neighbour(1, 0))
    rb = send(top, neighbour(-1, 0))
    return gl, gr, rl, rr, rt, rb


def add_split(shape, parts, *arrays):
    count = len(arrays)
    rows = shape[0] // parts

    def kernel(*refs):
        ins, outs = refs[:count], refs[count:]
        for k, out in enumerate(outs):
            value = ins[0][k * rows : (k + 1) * rows]
            for ref in ins[1:]:
                value = value + ref[k * rows : (k + 1) * rows]
            out[...] = value

    return vmem_call(kernel, "add_split", [(rows, *shape[1:])] * parts, [], *arrays)


def join(*arrays):
    rows = arrays[0].shape[0]

    def kernel(*refs):
        for k, ref in enumerate(refs[:-1]):
            refs[-1][k * rows : (k + 1) * rows] = ref[...]

    shape = (rows * len(arrays), *arrays[0].shape[1:])
    return vmem_call(kernel, "join", [shape], [], *arrays)[0]


def total_over_devices(keep, sent):
    arrived = send(sent, core_swap())
    parts = add_split((16, 24, PW), 4, keep, arrived)
    arrived = [send(parts[k], along_x(k)) for k in (1, 2, 3)]
    parts = add_split((4, 24, PW), 4, parts[0], *arrived)
    arrived = [send(parts[k], along_y(k)) for k in (1, 2, 3)]
    value = add_split((1, 24, PW), 1, parts[0], *arrived)[0]
    for k in (1, 2, 4):
        value = add_split((1, 24, PW), 1, value, send(value, along_z(k)))[0]
    value = join(value, *[send(value, along_y(k)) for k in (1, 2, 3)])
    value = join(value, *[send(value, along_x(k)) for k in (1, 2, 3)])
    return value, send(value, core_swap())


def first_windows(current):
    def packed(half):
        return jnp.concatenate([half[:, : PW // 2], half[:, PW // 2 :]], axis=2)

    def unpacked(value):
        return jnp.concatenate([value[:, :, :HALO], value[:, :, HALO:]], axis=1)

    left = unpacked(send(packed(current[:, :, TILE_W - HALO :]), neighbour(0, 1)))
    right = unpacked(send(packed(current[:, :, :HALO]), neighbour(0, -1)))
    wide = jnp.concatenate([left, current, right], axis=2)
    top = send(wide[:, PW - HALO :], neighbour(1, 0))
    bottom = send(wide[:, :HALO], neighbour(-1, 0))
    return jnp.concatenate([top, wide, bottom], axis=1)


def per_device(positions, row_offsets, amplitudes, object_field, probe_field):
    tables = dft_tables()
    s, t = lax.axis_index("stripe"), lax.axis_index("tile")
    core, x, y = s % 2, (t % 2) * 2 + (s // 2) % 2, t // 2
    offset = row_offsets[0, 2] + HALO
    third = jnp.minimum(offset // 8, 15) * 8
    where = jnp.stack([third, s, t, core, x, y, offset - third]).astype(jnp.int32)
    amp = amplitudes[0]
    probe = probe_field

    obj = first_windows(object_field)
    gl, gr, obj, probe, _ = run_pass(where, obj, None, probe, None, amp, tables, False)
    parts = exchange(gl, gr)
    gl, gr, obj, probe, rest = run_pass(where, obj, parts, probe, None, amp, tables, True)
    parts = exchange(gl, gr)
    sums = total_over_devices(*rest)
    gl, gr, obj, probe, _ = run_pass(where, obj, parts, probe, sums, amp, tables, False)
    parts = exchange(gl, gr)
    gl, gr, obj, probe, rest = run_pass(where, obj, parts, probe, None, amp, tables, True)
    parts = exchange(gl, gr)
    sums = total_over_devices(*rest)
    scratch = [pltpu.VMEM((2, EXT, PW), F32)]
    args = (where, obj, *parts, probe)
    object_out = vmem_call(object_kernel, "object_out", [(2, PW, TILE_W)], scratch, *args)[0]
    scratch = [pltpu.VMEM((3, PW, PW), F32)]
    probe_out = vmem_call(probe_kernel, "probe_out", [(2, PW, PW)], scratch, where, probe, *sums)[0]
    return object_out, probe_out


def solution(mesh):
    placed = (
        P("stripe", "tile"),
        P("stripe", "tile"),
        P("stripe", "tile", None, None),
        P(None, "stripe", "tile"),
        P(),
    )
    return jax.shard_map(
        per_device,
        mesh=mesh,
        in_specs=placed,
        out_specs=(P(None, "stripe", "tile"), P()),
        check_vma=False,
    )
```

```python
import functools
import math

import jax
import jax.numpy as jnp
from jax import lax
from jax.experimental import pallas as pl
from jax.experimental.pallas import tpu as pltpu
from jax.sharding import PartitionSpec as P

PW = 256
HALO = 64
TILE_W = 128
PAT_DEV = 3
STRIPES = 32
TILES = 8
EXT = PW + 2 * HALO
LANES = 128
AXES = ("stripe", "tile")
F32 = jnp.float32
BF16 = jnp.bfloat16


def place(x, y, z, core):
    return (z * 4 + (x % 2) * 2 + core) * TILES + y * 2 + x // 2


def physical(flat):
    s, t = flat // TILES, flat % TILES
    return (t % 2) * 2 + (s // 2) % 2, t // 2, s // 4, s % 2


def moved(step):
    pairs = []
    for flat in range(STRIPES * TILES):
        pairs.append((flat, place(*step(*physical(flat)))))
    return pairs


def core_swap():
    return moved(lambda x, y, z, c: (x, y, z, 1 - c))


def along_x(k):
    return moved(lambda x, y, z, c: ((x + k) % 4, y, z, c))


def along_y(k):
    return moved(lambda x, y, z, c: (x, (y + k) % 4, z, c))


def along_z(k):
    return moved(lambda x, y, z, c: (x, y, z ^ k, c))


def neighbour(ds, dt):
    pairs = []
    for s in range(STRIPES):
        for t in range(TILES):
            s2, t2 = s + ds, t + dt
            if 0 <= s2 < STRIPES and 0 <= t2 < TILES:
                pairs.append((s * TILES + t, s2 * TILES + t2))
    return pairs


def send(value, pairs):
    return lax.ppermute(value, AXES, pairs)


def dft_tables():
    indices = jnp.arange(PW, dtype=jnp.int32)
    phase = indices[:, None] * indices[None, :] % PW
    angles = phase.astype(jnp.float32) * (2.0 * math.pi / PW)
    factor = 1.0 / math.sqrt(PW)
    cosine = (jnp.cos(angles) * factor).astype(jnp.bfloat16)
    sine = (jnp.sin(angles) * factor).astype(jnp.bfloat16)
    forward = jnp.concatenate(
        [jnp.concatenate([cosine, sine], 1), jnp.concatenate([-sine, cosine], 1)], 0
    )
    inverse = jnp.concatenate(
        [jnp.concatenate([cosine, -sine], 1), jnp.concatenate([sine, cosine], 1)], 0
    )
    return forward, inverse


def vmem_call(kernel, name, out_shapes, scratch, *args, held=True, grant=8 << 20):
    smem = pl.BlockSpec(memory_space=pltpu.SMEM)
    vmem = pl.BlockSpec(memory_space=pltpu.VMEM)
    keep = pltpu.with_memory_space_constraint
    args = [a if a.dtype == jnp.int32 else keep(a, pltpu.VMEM) for a in args]
    return pl.pallas_call(
        kernel,
        name=name,
        in_specs=[smem if a.dtype == jnp.int32 else vmem for a in args],
        out_specs=[vmem for _ in out_shapes],
        out_shape=[pltpu.VMEM(s, F32) if held else jax.ShapeDtypeStruct(s, F32) for s in out_shapes],
        scratch_shapes=scratch,
        compiler_params=pltpu.CompilerParams(vmem_limit_bytes=grant),
    )(*args)


def step_of(probe_ref):
    power = probe_ref[0] * probe_ref[0] + probe_ref[1] * probe_ref[1]
    return 1.0 / (2.0 * PAT_DEV * jnp.max(power) + 1e-06)


def updated(place_ref, probe_ref, obj_ref, parts, store, rows, lanes):
    gl, gr, rl, rr, rt, rb = parts
    step = step_of(probe_ref)
    s, t = place_ref[1], place_ref[2]
    row_lo = jnp.where(s == 0, HALO, 0)
    row_hi = jnp.where(s == STRIPES - 1, HALO + PW, EXT)
    col_lo = jnp.where(t == 0, HALO, 0)
    col_hi = jnp.where(t == TILES - 1, HALO + TILE_W, PW)
    for side, own, other in ((0, gl, rl), (1, gr, rr)):
        cols = slice(side * LANES, (side + 1) * LANES)
        row = lax.broadcasted_iota(jnp.int32, (LANES, LANES), 0)
        col = lax.broadcasted_iota(jnp.int32, (LANES, LANES), 1) + side * LANES
        col_ok = (col >= col_lo) & (col < col_hi)
        for block in range(3):
            span = slice(block * LANES, (block + 1) * LANES)
            at = row + block * LANES
            ok = col_ok & (at >= row_lo) & (at < row_hi)
            factor = jnp.where(ok, step, 0.0)
            for ch in range(2):
                g = own[ch, span, :] + other[ch, span, :]
                if block == 0:
                    g = g + rt[ch, :, cols]
                if block == 2:
                    g = g + rb[ch, :, cols]
                store(ch, block, side, obj_ref[ch, span, cols] - factor * g)


def new_probe(place_ref, probe_ref, near_ref, far_ref, total_ref, out_ref):
    c, x, y = place_ref[3], place_ref[4], place_ref[5]
    for k in range(4):
        for j in range(4):
            block = ((x + 4 - k) % 4) * 4 + (y + 4 - j) % 4
            for half, ref in ((c, near_ref), (1 - c, far_ref)):
                row = pl.multiple_of((half * 16 + block) * 8, 8)
                for ch in range(3):
                    total_ref[ch, pl.ds(row, 8), :] = ref[k * 4 + j, ch * 8 : ch * 8 + 8, :]
    scale = 0.5 / (total_ref[2] + 1.0)
    for ch in range(2):
        out_ref[ch] = probe_ref[ch] - total_ref[ch] * scale


def lifted(value, shift):
    tiles = value.reshape(PW // 8 + 1, 8, value.shape[1])
    tiles = pltpu.roll(tiles, (8 - shift) % 8, axis=1)
    row = lax.broadcasted_iota(jnp.int32, (PW // 8, 8, value.shape[1]), 1)
    return jnp.where(row < 8 - shift, tiles[:-1], tiles[1:]).reshape(PW, value.shape[1])


def lowered(value, shift):
    tiles = value.reshape(PW // 8, 8, value.shape[1])
    tiles = pltpu.roll(tiles, shift % 8, axis=1)
    none = jnp.zeros((1, 8, value.shape[1]), F32)
    row = lax.broadcasted_iota(jnp.int32, (PW // 8 + 1, 8, value.shape[1]), 1)
    below = jnp.concatenate([tiles, none], axis=0)
    above = jnp.concatenate([none, tiles], axis=0)
    return jnp.where(row >= shift, below, above).reshape(PW + 8, value.shape[1])


def patterns(place_ref, obj_ref, probe_ref, amp_ref, fwd_ref, inv_ref, gl_ref, gr_ref, pg_ref):
    fwd, inv = fwd_ref[...], inv_ref[...]
    third, shift = pl.multiple_of(place_ref[0], 8), place_ref[6]
    for p in range(PAT_DEV):
        if p < 2:
            rows = pl.ds((0, 2 * HALO)[p], PW)
            wr, wi = obj_ref[0, rows, :], obj_ref[1, rows, :]
        else:
            wr, wi = [lifted(obj_ref[ch, pl.ds(third, PW + 8), :], shift) for ch in range(2)]
        pr, pi = probe_ref[0], probe_ref[1]
        exit_wave = jnp.concatenate(
            [(pr * wr - pi * wi).astype(BF16), (pr * wi + pi * wr).astype(BF16)], axis=0
        )
        half = jnp.dot(fwd, exit_wave, preferred_element_type=F32)
        half = jnp.concatenate([half[:PW].astype(BF16), half[PW:].astype(BF16)], axis=1)
        spec = jnp.dot(half, inv, preferred_element_type=F32)
        sr, si = spec[:, :PW], spec[:, PW:]
        scaling = amp_ref[p] * lax.rsqrt(jnp.maximum(sr * sr + si * si, 0.25))
        miss = jnp.concatenate(
            [(sr - scaling * sr).astype(BF16), (si - scaling * si).astype(BF16)], axis=0
        )
        half = jnp.dot(inv, miss, preferred_element_type=F32)
        half = jnp.concatenate([half[:PW].astype(BF16), half[PW:].astype(BF16)], axis=1)
        back = jnp.dot(half, fwd, preferred_element_type=F32)
        br, bi = back[:, :PW], back[:, PW:]
        for ch, og in ((0, pr * br + pi * bi), (1, pr * bi - pi * br)):
            for ref, part in ((gl_ref, og[:, :LANES]), (gr_ref, og[:, LANES:])):
                if p == 0:
                    ref[ch, 0:PW, :] = part
                elif p == 1:
                    ref[ch, 2 * HALO : PW, :] += part[: 2 * HALO]
                    ref[ch, PW:EXT, :] = part[2 * HALO :]
                else:
                    ref[ch, pl.ds(third, PW + 8), :] += lowered(part, shift)
        if pg_ref is not None:
            sums = (wr * br + wi * bi, wr * bi - wi * br, wr * wr + wi * wi)
            for ch, value in enumerate(sums):
                if p == 0:
                    pg_ref[ch] = value
                else:
                    pg_ref[ch] += value


def split_probe_grad(place_ref, pg_ref, keep_ref, send_ref):
    c, x, y = place_ref[3], place_ref[4], place_ref[5]
    for k in range(4):
        for j in range(4):
            block = ((x + k) % 4) * 4 + (y + j) % 4
            for half, ref in ((c, keep_ref), (1 - c, send_ref)):
                row = pl.multiple_of((half * 16 + block) * 8, 8)
                for ch in range(3):
                    ref[k * 4 + j, ch * 8 : ch * 8 + 8, :] = pg_ref[ch, pl.ds(row, 8), :]


def pass_kernel(first, last_inner, fresh_probe, *refs):
    refs = list(refs)
    place_ref = refs.pop(0)
    obj_ref = refs.pop(0)
    parts = None if first else [refs.pop(0) for _ in range(6)]
    probe_ref = refs.pop(0)
    sums = [refs.pop(0) for _ in range(2)] if fresh_probe else None
    amp_ref, fwd_ref, inv_ref = [refs.pop(0) for _ in range(3)]
    gl_ref, gr_ref = [refs.pop(0) for _ in range(2)]
    if not first:
        out_ref = refs.pop(0)

        def store(ch, block, side, value):
            rows = slice(block * LANES, (block + 1) * LANES)
            out_ref[ch, rows, side * LANES : (side + 1) * LANES] = value

        updated(place_ref, probe_ref, obj_ref, parts, store, None, None)
        obj_ref = out_ref
    if fresh_probe:
        fresh_ref = refs.pop(0)
    if last_inner:
        keep_ref, send_ref = [refs.pop(0) for _ in range(2)]
    if fresh_probe:
        new_probe(place_ref, probe_ref, sums[0], sums[1], refs[-1], fresh_ref)
        probe_ref = fresh_ref
    pg_ref = refs[-1] if last_inner else None
    patterns(place_ref, obj_ref, probe_ref, amp_ref, fwd_ref, inv_ref, gl_ref, gr_ref, pg_ref)
    if last_inner:
        split_probe_grad(place_ref, pg_ref, keep_ref, send_ref)


def run_pass(where, obj, parts, probe, sums, amp, tables, last_inner):
    first, fresh = parts is None, sums is not None
    args = [where, obj] + ([] if first else list(parts)) + [probe]
    args += (list(sums) if fresh else []) + [amp, *tables]
    outs = [(2, EXT, LANES)] * 2
    outs += [] if first else [(2, EXT, PW)]
    outs += [(2, PW, PW)] if fresh else []
    outs += [(16, 24, PW)] * 2 if last_inner else []
    scratch = [pltpu.VMEM((3, PW, PW), F32)] if fresh or last_inner else []
    kernel = functools.partial(pass_kernel, first, last_inner, fresh)
    got = list(vmem_call(kernel, "object_pass", outs, scratch, *args, grant=24 << 20))
    gl, gr = got.pop(0), got.pop(0)
    obj = obj if first else got.pop(0)
    probe = got.pop(0) if fresh else probe
    return gl, gr, obj, probe, got


def object_kernel(place_ref, obj_ref, gl, gr, rl, rr, rt, rb, probe_ref, out_ref, tmp_ref):
    def store(ch, block, side, value):
        rows = slice(block * LANES, (block + 1) * LANES)
        tmp_ref[ch, rows, side * LANES : (side + 1) * LANES] = value

    updated(place_ref, probe_ref, obj_ref, (gl, gr, rl, rr, rt, rb), store, None, None)
    out_ref[...] = tmp_ref[:, HALO : HALO + PW, HALO : HALO + TILE_W]


def probe_kernel(place_ref, probe_ref, near_ref, far_ref, out_ref, total_ref):
    new_probe(place_ref, probe_ref, near_ref, far_ref, total_ref, out_ref)


def exchange(gl, gr):
    rl = send(gr, neighbour(0, 1))
    rr = send(gl, neighbour(0, -1))

    def edges(gl, gr, rl, rr, top, bottom):
        for ch in range(2):
            for cols, a, b in ((slice(0, LANES), gl, rl), (slice(LANES, PW), gr, rr)):
                top[ch, :, cols] = a[ch, 0:LANES, :] + b[ch, 0:LANES, :]
                bottom[ch, :, cols] = a[ch, PW:EXT, :] + b[ch, PW:EXT, :]

    top, bottom = vmem_call(edges, "edges", [(2, LANES, PW)] * 2, [], gl, gr, rl, rr)
    rt = send(bottom, neighbour(1, 0))
    rb = send(top, neighbour(-1, 0))
    return gl, gr, rl, rr, rt, rb


def add_split(shape, parts, *arrays):
    count = len(arrays)
    rows = shape[0] // parts

    def kernel(*refs):
        ins, outs = refs[:count], refs[count:]
        for k, out in enumerate(outs):
            value = ins[0][k * rows : (k + 1) * rows]
            for ref in ins[1:]:
                value = value + ref[k * rows : (k + 1) * rows]
            out[...] = value

    return vmem_call(kernel, "add_split", [(rows, *shape[1:])] * parts, [], *arrays)


def join(*arrays):
    rows = arrays[0].shape[0]

    def kernel(*refs):
        for k, ref in enumerate(refs[:-1]):
            refs[-1][k * rows : (k + 1) * rows] = ref[...]

    shape = (rows * len(arrays), *arrays[0].shape[1:])
    return vmem_call(kernel, "join", [shape], [], *arrays)[0]


def total_over_devices(keep, sent):
    arrived = send(sent, core_swap())
    parts = add_split((16, 24, PW), 4, keep, arrived)
    arrived = [send(parts[k], along_x(k)) for k in (1, 2, 3)]
    parts = add_split((4, 24, PW), 4, parts[0], *arrived)
    arrived = [send(parts[k], along_y(k)) for k in (1, 2, 3)]
    value = add_split((1, 24, PW), 1, parts[0], *arrived)[0]
    for k in (1, 2, 4):
        value = add_split((1, 24, PW), 1, value, send(value, along_z(k)))[0]
    value = join(value, *[send(value, along_y(k)) for k in (1, 2, 3)])
    value = join(value, *[send(value, along_x(k)) for k in (1, 2, 3)])
    return value, send(value, core_swap())


def first_windows(current):
    def packed(half):
        return jnp.concatenate([half[:, : PW // 2], half[:, PW // 2 :]], axis=2)

    def unpacked(value):
        return jnp.concatenate([value[:, :, :HALO], value[:, :, HALO:]], axis=1)

    left = unpacked(send(packed(current[:, :, TILE_W - HALO :]), neighbour(0, 1)))
    right = unpacked(send(packed(current[:, :, :HALO]), neighbour(0, -1)))
    wide = jnp.concatenate([left, current, right], axis=2)
    top = send(wide[:, PW - HALO :], neighbour(1, 0))
    bottom = send(wide[:, :HALO], neighbour(-1, 0))
    return jnp.concatenate([top, wide, bottom], axis=1)


def per_device(positions, row_offsets, amplitudes, object_field, probe_field):
    tables = dft_tables()
    s, t = lax.axis_index("stripe"), lax.axis_index("tile")
    core, x, y = s % 2, (t % 2) * 2 + (s // 2) % 2, t // 2
    offset = row_offsets[0, 2] + HALO
    third = jnp.minimum(offset // 8, 15) * 8
    where = jnp.stack([third, s, t, core, x, y, offset - third]).astype(jnp.int32)
    amp = amplitudes[0]
    probe = probe_field

    obj = first_windows(object_field)
    gl, gr, obj, probe, _ = run_pass(where, obj, None, probe, None, amp, tables, False)
    parts = exchange(gl, gr)
    gl, gr, obj, probe, rest = run_pass(where, obj, parts, probe, None, amp, tables, True)
    parts = exchange(gl, gr)
    sums = total_over_devices(*rest)
    gl, gr, obj, probe, _ = run_pass(where, obj, parts, probe, sums, amp, tables, False)
    parts = exchange(gl, gr)
    gl, gr, obj, probe, rest = run_pass(where, obj, parts, probe, None, amp, tables, True)
    parts = exchange(gl, gr)
    sums = total_over_devices(*rest)
    scratch = [pltpu.VMEM((2, EXT, PW), F32)]
    args = (where, obj, *parts, probe)
    object_out = vmem_call(object_kernel, "object_out", [(2, PW, TILE_W)], scratch, *args, held=False)[0]
    scratch, args = [pltpu.VMEM((3, PW, PW), F32)], (where, probe, *sums)
    probe_out = vmem_call(probe_kernel, "probe_out", [(2, PW, PW)], scratch, *args, held=False)[0]
    return object_out, probe_out


def solution(mesh):
    placed = (
        P("stripe", "tile"),
        P("stripe", "tile"),
        P("stripe", "tile", None, None),
        P(None, "stripe", "tile"),
        P(),
    )
    return jax.shard_map(
        per_device,
        mesh=mesh,
        in_specs=placed,
        out_specs=(P(None, "stripe", "tile"), P()),
        check_vma=False,
    )
```

```python
import functools
import math

import jax
import jax.numpy as jnp
from jax import lax
from jax.experimental import pallas as pl
from jax.experimental.pallas import tpu as pltpu
from jax.sharding import PartitionSpec as P

PW = 256
HALO = 64
TILE_W = 128
PAT_DEV = 3
STRIPES = 32
TILES = 8
EXT = PW + 2 * HALO
LANES = 128
AXES = ("stripe", "tile")
F32 = jnp.float32
BF16 = jnp.bfloat16


def place(x, y, z, core):
    return (z * 4 + (x % 2) * 2 + core) * TILES + y * 2 + x // 2


def physical(flat):
    s, t = flat // TILES, flat % TILES
    return (t % 2) * 2 + (s // 2) % 2, t // 2, s // 4, s % 2


def moved(step):
    pairs = []
    for flat in range(STRIPES * TILES):
        pairs.append((flat, place(*step(*physical(flat)))))
    return pairs


def core_swap():
    return moved(lambda x, y, z, c: (x, y, z, 1 - c))


def along_x(k):
    return moved(lambda x, y, z, c: ((x + k) % 4, y, z, c))


def along_y(k):
    return moved(lambda x, y, z, c: (x, (y + k) % 4, z, c))


def along_z(k):
    return moved(lambda x, y, z, c: (x, y, z ^ k, c))


def host(s, t):
    return place(s % 4, t // 2, s // 4, t % 2)


def to_host():
    return [(s * TILES + t, host(s, t)) for s in range(STRIPES) for t in range(TILES)]


def from_host():
    return [(there, here) for here, there in to_host()]


def neighbour(ds, dt):
    pairs = []
    for s in range(STRIPES):
        for t in range(TILES):
            s2, t2 = s + ds, t + dt
            if 0 <= s2 < STRIPES and 0 <= t2 < TILES:
                pairs.append((host(s, t), host(s2, t2)))
    return pairs


def send(value, pairs):
    return lax.ppermute(value, AXES, pairs)


def dft_tables():
    indices = jnp.arange(PW, dtype=jnp.int32)
    phase = indices[:, None] * indices[None, :] % PW
    angles = phase.astype(jnp.float32) * (2.0 * math.pi / PW)
    factor = 1.0 / math.sqrt(PW)
    cosine = (jnp.cos(angles) * factor).astype(jnp.bfloat16)
    sine = (jnp.sin(angles) * factor).astype(jnp.bfloat16)
    forward = jnp.concatenate(
        [jnp.concatenate([cosine, sine], 1), jnp.concatenate([-sine, cosine], 1)], 0
    )
    inverse = jnp.concatenate(
        [jnp.concatenate([cosine, -sine], 1), jnp.concatenate([sine, cosine], 1)], 0
    )
    return forward, inverse


def vmem_call(kernel, name, out_shapes, scratch, *args, held=True, grant=8 << 20):
    smem = pl.BlockSpec(memory_space=pltpu.SMEM)
    vmem = pl.BlockSpec(memory_space=pltpu.VMEM)
    keep = pltpu.with_memory_space_constraint
    args = [a if a.dtype == jnp.int32 else keep(a, pltpu.VMEM) for a in args]
    return pl.pallas_call(
        kernel,
        name=name,
        in_specs=[smem if a.dtype == jnp.int32 else vmem for a in args],
        out_specs=[vmem for _ in out_shapes],
        out_shape=[pltpu.VMEM(s, F32) if held else jax.ShapeDtypeStruct(s, F32) for s in out_shapes],
        scratch_shapes=scratch,
        compiler_params=pltpu.CompilerParams(vmem_limit_bytes=grant),
    )(*args)


def step_of(probe_ref):
    power = probe_ref[0] * probe_ref[0] + probe_ref[1] * probe_ref[1]
    return 1.0 / (2.0 * PAT_DEV * jnp.max(power) + 1e-06)


def updated(place_ref, probe_ref, obj_ref, parts, store, rows, lanes):
    gl, gr, rl, rr, rt, rb = parts
    step = step_of(probe_ref)
    s, t = place_ref[1], place_ref[2]
    row_lo = jnp.where(s == 0, HALO, 0)
    row_hi = jnp.where(s == STRIPES - 1, HALO + PW, EXT)
    col_lo = jnp.where(t == 0, HALO, 0)
    col_hi = jnp.where(t == TILES - 1, HALO + TILE_W, PW)
    for side, own, other in ((0, gl, rl), (1, gr, rr)):
        cols = slice(side * LANES, (side + 1) * LANES)
        row = lax.broadcasted_iota(jnp.int32, (LANES, LANES), 0)
        col = lax.broadcasted_iota(jnp.int32, (LANES, LANES), 1) + side * LANES
        col_ok = (col >= col_lo) & (col < col_hi)
        for block in range(3):
            span = slice(block * LANES, (block + 1) * LANES)
            at = row + block * LANES
            ok = col_ok & (at >= row_lo) & (at < row_hi)
            factor = jnp.where(ok, step, 0.0)
            for ch in range(2):
                g = own[ch, span, :] + other[ch, span, :]
                if block == 0:
                    g = g + rt[ch, :, cols]
                if block == 2:
                    g = g + rb[ch, :, cols]
                store(ch, block, side, obj_ref[ch, span, cols] - factor * g)


def new_probe(place_ref, probe_ref, near_ref, far_ref, total_ref, out_ref):
    c, x, y = place_ref[3], place_ref[4], place_ref[5]
    for k in range(4):
        for j in range(4):
            block = ((x + 4 - k) % 4) * 4 + (y + 4 - j) % 4
            for half, ref in ((c, near_ref), (1 - c, far_ref)):
                row = pl.multiple_of((half * 16 + block) * 8, 8)
                for ch in range(3):
                    total_ref[ch, pl.ds(row, 8), :] = ref[k * 4 + j, ch * 8 : ch * 8 + 8, :]
    scale = 0.5 / (total_ref[2] + 1.0)
    for ch in range(2):
        out_ref[ch] = probe_ref[ch] - total_ref[ch] * scale


def lifted(value, shift):
    tiles = value.reshape(PW // 8 + 1, 8, value.shape[1])
    tiles = pltpu.roll(tiles, (8 - shift) % 8, axis=1)
    row = lax.broadcasted_iota(jnp.int32, (PW // 8, 8, value.shape[1]), 1)
    return jnp.where(row < 8 - shift, tiles[:-1], tiles[1:]).reshape(PW, value.shape[1])


def lowered(value, shift):
    tiles = value.reshape(PW // 8, 8, value.shape[1])
    tiles = pltpu.roll(tiles, shift % 8, axis=1)
    none = jnp.zeros((1, 8, value.shape[1]), F32)
    row = lax.broadcasted_iota(jnp.int32, (PW // 8 + 1, 8, value.shape[1]), 1)
    below = jnp.concatenate([tiles, none], axis=0)
    above = jnp.concatenate([none, tiles], axis=0)
    return jnp.where(row >= shift, below, above).reshape(PW + 8, value.shape[1])


def patterns(place_ref, obj_ref, probe_ref, amp_ref, fwd_ref, inv_ref, gl_ref, gr_ref, pg_ref):
    fwd, inv = fwd_ref[...], inv_ref[...]
    third, shift = pl.multiple_of(place_ref[0], 8), place_ref[6]
    for p in range(PAT_DEV):
        if p < 2:
            rows = pl.ds((0, 2 * HALO)[p], PW)
            wr, wi = obj_ref[0, rows, :], obj_ref[1, rows, :]
        else:
            wr, wi = [lifted(obj_ref[ch, pl.ds(third, PW + 8), :], shift) for ch in range(2)]
        pr, pi = probe_ref[0], probe_ref[1]
        exit_wave = jnp.concatenate(
            [(pr * wr - pi * wi).astype(BF16), (pr * wi + pi * wr).astype(BF16)], axis=0
        )
        half = jnp.dot(fwd, exit_wave, preferred_element_type=F32)
        half = jnp.concatenate([half[:PW].astype(BF16), half[PW:].astype(BF16)], axis=1)
        spec = jnp.dot(half, inv, preferred_element_type=F32)
        sr, si = spec[:, :PW], spec[:, PW:]
        scaling = amp_ref[p] * lax.rsqrt(jnp.maximum(sr * sr + si * si, 0.25))
        miss = jnp.concatenate(
            [(sr - scaling * sr).astype(BF16), (si - scaling * si).astype(BF16)], axis=0
        )
        half = jnp.dot(inv, miss, preferred_element_type=F32)
        half = jnp.concatenate([half[:PW].astype(BF16), half[PW:].astype(BF16)], axis=1)
        back = jnp.dot(half, fwd, preferred_element_type=F32)
        br, bi = back[:, :PW], back[:, PW:]
        for ch, og in ((0, pr * br + pi * bi), (1, pr * bi - pi * br)):
            for ref, part in ((gl_ref, og[:, :LANES]), (gr_ref, og[:, LANES:])):
                if p == 0:
                    ref[ch, 0:PW, :] = part
                elif p == 1:
                    ref[ch, 2 * HALO : PW, :] += part[: 2 * HALO]
                    ref[ch, PW:EXT, :] = part[2 * HALO :]
                else:
                    ref[ch, pl.ds(third, PW + 8), :] += lowered(part, shift)
        if pg_ref is not None:
            sums = (wr * br + wi * bi, wr * bi - wi * br, wr * wr + wi * wi)
            for ch, value in enumerate(sums):
                if p == 0:
                    pg_ref[ch] = value
                else:
                    pg_ref[ch] += value


def split_probe_grad(place_ref, pg_ref, keep_ref, send_ref):
    c, x, y = place_ref[3], place_ref[4], place_ref[5]
    for k in range(4):
        for j in range(4):
            block = ((x + k) % 4) * 4 + (y + j) % 4
            for half, ref in ((c, keep_ref), (1 - c, send_ref)):
                row = pl.multiple_of((half * 16 + block) * 8, 8)
                for ch in range(3):
                    ref[k * 4 + j, ch * 8 : ch * 8 + 8, :] = pg_ref[ch, pl.ds(row, 8), :]


def pass_kernel(first, last_inner, fresh_probe, *refs):
    refs = list(refs)
    place_ref = refs.pop(0)
    obj_ref = refs.pop(0)
    parts = None if first else [refs.pop(0) for _ in range(6)]
    probe_ref = refs.pop(0)
    sums = [refs.pop(0) for _ in range(2)] if fresh_probe else None
    amp_ref, fwd_ref, inv_ref = [refs.pop(0) for _ in range(3)]
    gl_ref, gr_ref = [refs.pop(0) for _ in range(2)]
    if not first:
        out_ref = refs.pop(0)

        def store(ch, block, side, value):
            rows = slice(block * LANES, (block + 1) * LANES)
            out_ref[ch, rows, side * LANES : (side + 1) * LANES] = value

        updated(place_ref, probe_ref, obj_ref, parts, store, None, None)
        obj_ref = out_ref
    if fresh_probe:
        fresh_ref = refs.pop(0)
    if last_inner:
        keep_ref, send_ref = [refs.pop(0) for _ in range(2)]
    if fresh_probe:
        new_probe(place_ref, probe_ref, sums[0], sums[1], refs[-1], fresh_ref)
        probe_ref = fresh_ref
    pg_ref = refs[-1] if last_inner else None
    patterns(place_ref, obj_ref, probe_ref, amp_ref, fwd_ref, inv_ref, gl_ref, gr_ref, pg_ref)
    if last_inner:
        split_probe_grad(place_ref, pg_ref, keep_ref, send_ref)


def run_pass(where, obj, parts, probe, sums, amp, tables, last_inner):
    first, fresh = parts is None, sums is not None
    args = [where, obj] + ([] if first else list(parts)) + [probe]
    args += (list(sums) if fresh else []) + [amp, *tables]
    outs = [(2, EXT, LANES)] * 2
    outs += [] if first else [(2, EXT, PW)]
    outs += [(2, PW, PW)] if fresh else []
    outs += [(16, 24, PW)] * 2 if last_inner else []
    scratch = [pltpu.VMEM((3, PW, PW), F32)] if fresh or last_inner else []
    kernel = functools.partial(pass_kernel, first, last_inner, fresh)
    got = list(vmem_call(kernel, "object_pass", outs, scratch, *args, grant=24 << 20))
    gl, gr = got.pop(0), got.pop(0)
    obj = obj if first else got.pop(0)
    probe = got.pop(0) if fresh else probe
    return gl, gr, obj, probe, got


def object_kernel(place_ref, obj_ref, gl, gr, rl, rr, rt, rb, probe_ref, out_ref, tmp_ref):
    def store(ch, block, side, value):
        rows = slice(block * LANES, (block + 1) * LANES)
        tmp_ref[ch, rows, side * LANES : (side + 1) * LANES] = value

    updated(place_ref, probe_ref, obj_ref, (gl, gr, rl, rr, rt, rb), store, None, None)
    out_ref[...] = tmp_ref[:, HALO : HALO + PW, HALO : HALO + TILE_W]


def probe_kernel(place_ref, probe_ref, near_ref, far_ref, out_ref, total_ref):
    new_probe(place_ref, probe_ref, near_ref, far_ref, total_ref, out_ref)


def exchange_columns(gl, gr):
    return gl, gr, send(gr, neighbour(0, 1)), send(gl, neighbour(0, -1))


def exchange_rows(gl, gr, rl, rr):
    def edges(gl, gr, rl, rr, top, bottom):
        for ch in range(2):
            for cols, a, b in ((slice(0, LANES), gl, rl), (slice(LANES, PW), gr, rr)):
                top[ch, :, cols] = a[ch, 0:LANES, :] + b[ch, 0:LANES, :]
                bottom[ch, :, cols] = a[ch, PW:EXT, :] + b[ch, PW:EXT, :]

    top, bottom = vmem_call(edges, "edges", [(2, LANES, PW)] * 2, [], gl, gr, rl, rr)
    rt = send(bottom, neighbour(1, 0))
    rb = send(top, neighbour(-1, 0))
    return gl, gr, rl, rr, rt, rb


def add_split(shape, parts, *arrays):
    count = len(arrays)
    rows = shape[0] // parts

    def kernel(*refs):
        ins, outs = refs[:count], refs[count:]
        for k, out in enumerate(outs):
            value = ins[0][k * rows : (k + 1) * rows]
            for ref in ins[1:]:
                value = value + ref[k * rows : (k + 1) * rows]
            out[...] = value

    return vmem_call(kernel, "add_split", [(rows, *shape[1:])] * parts, [], *arrays)


def join(*arrays):
    rows = arrays[0].shape[0]

    def kernel(*refs):
        for k, ref in enumerate(refs[:-1]):
            refs[-1][k * rows : (k + 1) * rows] = ref[...]

    shape = (rows * len(arrays), *arrays[0].shape[1:])
    return vmem_call(kernel, "join", [shape], [], *arrays)[0]


def exchange(gl, gr):
    return exchange_rows(*exchange_columns(gl, gr))


def exchange_and_total(gl, gr, keep, sent):
    columns = exchange_columns(gl, gr)
    arrived = send(sent, core_swap())
    parts = add_split((16, 24, PW), 4, keep, arrived)
    arrived = [send(parts[k], along_x(k)) for k in (1, 2, 3)]
    arrived, columns = lax.optimization_barrier((arrived, columns))
    rows = exchange_rows(*columns)
    parts = add_split((4, 24, PW), 4, parts[0], *arrived)
    arrived = [send(parts[k], along_y(k)) for k in (1, 2, 3)]
    value = add_split((1, 24, PW), 1, parts[0], *arrived)[0]
    for k in (1, 2, 4):
        value = add_split((1, 24, PW), 1, value, send(value, along_z(k)))[0]
        if k == 1:
            value, rows = lax.optimization_barrier((value, rows))
    value = join(value, *[send(value, along_y(k)) for k in (1, 2, 3)])
    value = join(value, *[send(value, along_x(k)) for k in (1, 2, 3)])
    return rows, (value, send(value, core_swap()))


def first_windows(current):
    def packed(half):
        return jnp.concatenate([half[:, : PW // 2], half[:, PW // 2 :]], axis=2)

    def unpacked(value):
        return jnp.concatenate([value[:, :, :HALO], value[:, :, HALO:]], axis=1)

    left = unpacked(send(packed(current[:, :, TILE_W - HALO :]), neighbour(0, 1)))
    right = unpacked(send(packed(current[:, :, :HALO]), neighbour(0, -1)))
    wide = jnp.concatenate([left, current, right], axis=2)
    top = send(wide[:, PW - HALO :], neighbour(1, 0))
    bottom = send(wide[:, :HALO], neighbour(-1, 0))
    return jnp.concatenate([top, wide, bottom], axis=1)


def per_device(positions, row_offsets, amplitudes, object_field, probe_field):
    tables = dft_tables()
    stripe, tile = lax.axis_index("stripe"), lax.axis_index("tile")
    core, x, y, z = stripe % 2, (tile % 2) * 2 + (stripe // 2) % 2, tile // 2, stripe // 4
    current = send(object_field, to_host())
    amp = send(amplitudes[0], to_host())
    offset = send(row_offsets, to_host())[0, 2] + HALO
    third = jnp.minimum(offset // 8, 15) * 8
    place_of = [third, z * 4 + x, y * 2 + core, core, x, y, offset - third]
    where = jnp.stack(place_of).astype(jnp.int32)
    probe = probe_field

    obj = first_windows(current)
    gl, gr, obj, probe, _ = run_pass(where, obj, None, probe, None, amp, tables, False)
    parts = exchange(gl, gr)
    gl, gr, obj, probe, rest = run_pass(where, obj, parts, probe, None, amp, tables, True)
    parts, sums = exchange_and_total(gl, gr, *rest)
    gl, gr, obj, probe, _ = run_pass(where, obj, parts, probe, sums, amp, tables, False)
    parts = exchange(gl, gr)
    gl, gr, obj, probe, rest = run_pass(where, obj, parts, probe, None, amp, tables, True)
    parts, sums = exchange_and_total(gl, gr, *rest)
    scratch = [pltpu.VMEM((2, EXT, PW), F32)]
    args = (where, obj, *parts, probe)
    current = vmem_call(object_kernel, "object_out", [(2, PW, TILE_W)], scratch, *args)[0]
    object_out = send(current, from_host())
    scratch, args = [pltpu.VMEM((3, PW, PW), F32)], (where, probe, *sums)
    probe_out = vmem_call(probe_kernel, "probe_out", [(2, PW, PW)], scratch, *args, held=False)[0]
    return object_out, probe_out


def solution(mesh):
    placed = (
        P("stripe", "tile"),
        P("stripe", "tile"),
        P("stripe", "tile", None, None),
        P(None, "stripe", "tile"),
        P(),
    )
    return jax.shard_map(
        per_device,
        mesh=mesh,
        in_specs=placed,
        out_specs=(P(None, "stripe", "tile"), P()),
        check_vma=False,
    )
```

```python
import functools
import math

import jax
import jax.numpy as jnp
from jax import lax
from jax.experimental import pallas as pl
from jax.experimental.pallas import tpu as pltpu
from jax.sharding import PartitionSpec as P

PW = 256
HALO = 64
TILE_W = 128
PAT_DEV = 3
OUTER = 2
STRIPES = 32
TILES = 8
EXT = PW + 2 * HALO
LANES = 128
AXES = ("stripe", "tile")
F32 = jnp.float32
BF16 = jnp.bfloat16


def place(x, y, z, core):
    return (z * 4 + (x % 2) * 2 + core) * TILES + y * 2 + x // 2


def physical(flat):
    s, t = flat // TILES, flat % TILES
    return (t % 2) * 2 + (s // 2) % 2, t // 2, s // 4, s % 2


def moved(step):
    pairs = []
    for flat in range(STRIPES * TILES):
        pairs.append((flat, place(*step(*physical(flat)))))
    return pairs


def core_swap():
    return moved(lambda x, y, z, c: (x, y, z, 1 - c))


def along_x(k):
    return moved(lambda x, y, z, c: (x ^ k, y, z, c))


def along_y(k):
    return moved(lambda x, y, z, c: (x, y ^ k, z, c))


def along_z(k):
    return moved(lambda x, y, z, c: (x, y, z ^ k, c))


def host(s, t):
    return place(s % 4, t // 2, s // 4, t % 2)


def to_host():
    return [(s * TILES + t, host(s, t)) for s in range(STRIPES) for t in range(TILES)]


def from_host():
    return [(there, here) for here, there in to_host()]


def neighbour(ds, dt):
    pairs = []
    for s in range(STRIPES):
        for t in range(TILES):
            pairs.append((host(s, t), host((s + ds) % STRIPES, (t + dt) % TILES)))
    return pairs


def send(value, pairs):
    return lax.ppermute(value, AXES, pairs)


def dft_tables():
    indices = jnp.arange(PW, dtype=jnp.int32)
    phase = indices[:, None] * indices[None, :] % PW
    angles = phase.astype(jnp.float32) * (2.0 * math.pi / PW)
    factor = 1.0 / math.sqrt(PW)
    cosine = (jnp.cos(angles) * factor).astype(jnp.bfloat16)
    sine = (jnp.sin(angles) * factor).astype(jnp.bfloat16)
    forward = jnp.concatenate(
        [jnp.concatenate([cosine, sine], 1), jnp.concatenate([-sine, cosine], 1)], 0
    )
    inverse = jnp.concatenate(
        [jnp.concatenate([cosine, -sine], 1), jnp.concatenate([sine, cosine], 1)], 0
    )
    return forward, inverse


def vmem_call(kernel, name, out_shapes, scratch, *args, held=True, grant=8 << 20):
    smem = pl.BlockSpec(memory_space=pltpu.SMEM)
    vmem = pl.BlockSpec(memory_space=pltpu.VMEM)
    keep = pltpu.with_memory_space_constraint
    args = [a if a.dtype == jnp.int32 else keep(a, pltpu.VMEM) for a in args]
    return pl.pallas_call(
        kernel,
        name=name,
        in_specs=[smem if a.dtype == jnp.int32 else vmem for a in args],
        out_specs=[vmem for _ in out_shapes],
        out_shape=[pltpu.VMEM(s, F32) if held else jax.ShapeDtypeStruct(s, F32) for s in out_shapes],
        scratch_shapes=scratch,
        compiler_params=pltpu.CompilerParams(vmem_limit_bytes=grant),
    )(*args)


def unless(end, value):
    return jnp.where(end, jnp.zeros_like(value), value)


def step_of(probe_ref):
    power = probe_ref[0] * probe_ref[0] + probe_ref[1] * probe_ref[1]
    return 1.0 / (2.0 * PAT_DEV * jnp.max(power) + 1e-06)


def updated(place_ref, probe_ref, obj_ref, parts, store):
    gl, gr, rl, rr, rt, rb = parts
    step = step_of(probe_ref)
    s, t = place_ref[1], place_ref[2]
    row_lo = jnp.where(s == 0, HALO, 0)
    row_hi = jnp.where(s == STRIPES - 1, HALO + PW, EXT)
    col_lo = jnp.where(t == 0, HALO, 0)
    col_hi = jnp.where(t == TILES - 1, HALO + TILE_W, PW)
    for side, own, other, end in ((0, gl, rl, t == 0), (1, gr, rr, t == TILES - 1)):
        cols = slice(side * LANES, (side + 1) * LANES)
        row = lax.broadcasted_iota(jnp.int32, (LANES, LANES), 0)
        col = lax.broadcasted_iota(jnp.int32, (LANES, LANES), 1) + side * LANES
        col_ok = (col >= col_lo) & (col < col_hi)
        for block in range(3):
            span = slice(block * LANES, (block + 1) * LANES)
            at = row + block * LANES
            ok = col_ok & (at >= row_lo) & (at < row_hi)
            factor = jnp.where(ok, step, 0.0)
            for ch in range(2):
                g = own[ch, span, :] + unless(end, other[ch, span, :])
                if block == 0:
                    g = g + unless(s == 0, rt[ch, :, cols])
                if block == 2:
                    g = g + unless(s == STRIPES - 1, rb[ch, :, cols])
                store(ch, block, side, obj_ref[ch, span, cols] - factor * g)


def new_probe(place_ref, probe_ref, near_ref, far_ref, total_ref, out_ref):
    c, x, y = place_ref[3], place_ref[4], place_ref[5]
    for k in range(4):
        for j in range(4):
            block = (x ^ k) * 4 + (y ^ j)
            for half, ref in ((c, near_ref), (1 - c, far_ref)):
                row = pl.multiple_of((half * 16 + block) * 8, 8)
                for ch in range(3):
                    total_ref[ch, pl.ds(row, 8), :] = ref[k * 4 + j, ch * 8 : ch * 8 + 8, :]
    scale = 0.5 / (total_ref[2] + 1.0)
    for ch in range(2):
        out_ref[ch] = probe_ref[ch] - total_ref[ch] * scale


def lifted(value, shift):
    tiles = value.reshape(PW // 8 + 1, 8, value.shape[1])
    tiles = pltpu.roll(tiles, (8 - shift) % 8, axis=1)
    row = lax.broadcasted_iota(jnp.int32, (PW // 8, 8, value.shape[1]), 1)
    return jnp.where(row < 8 - shift, tiles[:-1], tiles[1:]).reshape(PW, value.shape[1])


def lowered(value, shift):
    tiles = value.reshape(PW // 8, 8, value.shape[1])
    tiles = pltpu.roll(tiles, shift % 8, axis=1)
    none = jnp.zeros((1, 8, value.shape[1]), F32)
    row = lax.broadcasted_iota(jnp.int32, (PW // 8 + 1, 8, value.shape[1]), 1)
    below = jnp.concatenate([tiles, none], axis=0)
    above = jnp.concatenate([none, tiles], axis=0)
    return jnp.where(row >= shift, below, above).reshape(PW + 8, value.shape[1])


def patterns(place_ref, obj_ref, probe_ref, amp_ref, fwd_ref, inv_ref, gl_ref, gr_ref, pg_ref):
    fwd, inv = fwd_ref[...], inv_ref[...]
    third, shift = pl.multiple_of(place_ref[0], 8), place_ref[6]
    for p in range(PAT_DEV):
        if p < 2:
            rows = pl.ds((0, 2 * HALO)[p], PW)
            wr, wi = obj_ref[0, rows, :], obj_ref[1, rows, :]
        else:
            wr, wi = [lifted(obj_ref[ch, pl.ds(third, PW + 8), :], shift) for ch in range(2)]
        pr, pi = probe_ref[0], probe_ref[1]
        exit_wave = jnp.concatenate(
            [(pr * wr - pi * wi).astype(BF16), (pr * wi + pi * wr).astype(BF16)], axis=0
        )
        half = jnp.dot(fwd, exit_wave, preferred_element_type=F32)
        half = jnp.concatenate([half[:PW].astype(BF16), half[PW:].astype(BF16)], axis=1)
        spec = jnp.dot(half, inv, preferred_element_type=F32)
        sr, si = spec[:, :PW], spec[:, PW:]
        scaling = amp_ref[p] * lax.rsqrt(jnp.maximum(sr * sr + si * si, 0.25))
        miss = jnp.concatenate(
            [(sr - scaling * sr).astype(BF16), (si - scaling * si).astype(BF16)], axis=0
        )
        half = jnp.dot(inv, miss, preferred_element_type=F32)
        half = jnp.concatenate([half[:PW].astype(BF16), half[PW:].astype(BF16)], axis=1)
        back = jnp.dot(half, fwd, preferred_element_type=F32)
        br, bi = back[:, :PW], back[:, PW:]
        for ch, og in ((0, pr * br + pi * bi), (1, pr * bi - pi * br)):
            for ref, part in ((gl_ref, og[:, :LANES]), (gr_ref, og[:, LANES:])):
                if p == 0:
                    ref[ch, 0:PW, :] = part
                elif p == 1:
                    ref[ch, 2 * HALO : PW, :] += part[: 2 * HALO]
                    ref[ch, PW:EXT, :] = part[2 * HALO :]
                else:
                    ref[ch, pl.ds(third, PW + 8), :] += lowered(part, shift)
        if pg_ref is not None:
            sums = (wr * br + wi * bi, wr * bi - wi * br, wr * wr + wi * wi)
            for ch, value in enumerate(sums):
                if p == 0:
                    pg_ref[ch] = value
                else:
                    pg_ref[ch] += value


def split_probe_grad(place_ref, pg_ref, keep_ref, send_ref):
    c, x, y = place_ref[3], place_ref[4], place_ref[5]
    for k in range(4):
        for j in range(4):
            block = (x ^ k) * 4 + (y ^ j)
            for half, ref in ((c, keep_ref), (1 - c, send_ref)):
                row = pl.multiple_of((half * 16 + block) * 8, 8)
                for ch in range(3):
                    ref[k * 4 + j, ch * 8 : ch * 8 + 8, :] = pg_ref[ch, pl.ds(row, 8), :]


def pass_kernel(first, last_inner, fresh_probe, *refs):
    refs = list(refs)
    place_ref = refs.pop(0)
    obj_ref = refs.pop(0)
    parts = None if first else [refs.pop(0) for _ in range(6)]
    probe_ref = refs.pop(0)
    sums = [refs.pop(0) for _ in range(2)] if fresh_probe else None
    amp_ref, fwd_ref, inv_ref = [refs.pop(0) for _ in range(3)]
    gl_ref, gr_ref = [refs.pop(0) for _ in range(2)]
    if not first:
        out_ref = refs.pop(0)

        def store(ch, block, side, value):
            rows = slice(block * LANES, (block + 1) * LANES)
            out_ref[ch, rows, side * LANES : (side + 1) * LANES] = value

        updated(place_ref, probe_ref, obj_ref, parts, store)
        obj_ref = out_ref
    if fresh_probe:
        fresh_ref = refs.pop(0)
    if last_inner:
        keep_ref, send_ref = [refs.pop(0) for _ in range(2)]
    if fresh_probe:
        new_probe(place_ref, probe_ref, sums[0], sums[1], refs[-1], fresh_ref)
        probe_ref = fresh_ref
    pg_ref = refs[-1] if last_inner else None
    patterns(place_ref, obj_ref, probe_ref, amp_ref, fwd_ref, inv_ref, gl_ref, gr_ref, pg_ref)
    if last_inner:
        split_probe_grad(place_ref, pg_ref, keep_ref, send_ref)


def run_pass(where, obj, parts, probe, sums, amp, tables, last_inner):
    first, fresh = parts is None, sums is not None
    args = [where, obj] + ([] if first else list(parts)) + [probe]
    args += (list(sums) if fresh else []) + [amp, *tables]
    outs = [(2, EXT, LANES)] * 2
    outs += [] if first else [(2, EXT, PW)]
    outs += [(2, PW, PW)] if fresh else []
    outs += [(16, 24, PW)] * 2 if last_inner else []
    scratch = [pltpu.VMEM((3, PW, PW), F32)] if fresh or last_inner else []
    kernel = functools.partial(pass_kernel, first, last_inner, fresh)
    got = list(vmem_call(kernel, "object_pass", outs, scratch, *args, grant=24 << 20))
    gl, gr = got.pop(0), got.pop(0)
    obj = obj if first else got.pop(0)
    probe = got.pop(0) if fresh else probe
    return gl, gr, obj, probe, got


def object_kernel(place_ref, obj_ref, gl, gr, rl, rr, rt, rb, probe_ref, out_ref, middle_ref):
    def store(ch, block, side, value):
        rows = slice(block * LANES, (block + 1) * LANES)
        out_ref[ch, rows, side * LANES : (side + 1) * LANES] = value

    updated(place_ref, probe_ref, obj_ref, (gl, gr, rl, rr, rt, rb), store)
    middle_ref[...] = out_ref[:, HALO : HALO + PW, HALO : HALO + TILE_W]


def probe_kernel(place_ref, probe_ref, near_ref, far_ref, out_ref, total_ref):
    new_probe(place_ref, probe_ref, near_ref, far_ref, total_ref, out_ref)


def exchange_columns(gl, gr):
    return gl, gr, send(gr, neighbour(0, 1)), send(gl, neighbour(0, -1))


def exchange_rows(where, gl, gr, rl, rr):
    def edges(place_ref, gl, gr, rl, rr, top, bottom):
        t = place_ref[2]
        halves = (slice(0, LANES), gl, rl, t == 0), (slice(LANES, PW), gr, rr, t == TILES - 1)
        for ch in range(2):
            for cols, a, b, end in halves:
                top[ch, :, cols] = a[ch, 0:LANES, :] + unless(end, b[ch, 0:LANES, :])
                bottom[ch, :, cols] = a[ch, PW:EXT, :] + unless(end, b[ch, PW:EXT, :])

    top, bottom = vmem_call(edges, "edges", [(2, LANES, PW)] * 2, [], where, gl, gr, rl, rr)
    rt = send(bottom, neighbour(1, 0))
    rb = send(top, neighbour(-1, 0))
    return gl, gr, rl, rr, rt, rb


def add_split(shape, parts, *arrays):
    count = len(arrays)
    rows = shape[0] // parts

    def kernel(*refs):
        ins, outs = refs[:count], refs[count:]
        for k, out in enumerate(outs):
            value = ins[0][k * rows : (k + 1) * rows]
            for ref in ins[1:]:
                value = value + ref[k * rows : (k + 1) * rows]
            out[...] = value

    return vmem_call(kernel, "add_split", [(rows, *shape[1:])] * parts, [], *arrays)


def join(*arrays):
    rows = arrays[0].shape[0]

    def kernel(*refs):
        for k, ref in enumerate(refs[:-1]):
            refs[-1][k * rows : (k + 1) * rows] = ref[...]

    shape = (rows * len(arrays), *arrays[0].shape[1:])
    return vmem_call(kernel, "join", [shape], [], *arrays)[0]


def exchange(where, gl, gr):
    return exchange_rows(where, *exchange_columns(gl, gr))


def exchange_and_total(where, obj, probe, gl, gr, keep, sent):
    columns = exchange_columns(gl, gr)
    arrived = send(sent, core_swap())
    parts = add_split((16, 24, PW), 4, keep, arrived)
    arrived = [send(parts[k], along_x(k)) for k in (1, 2, 3)]
    arrived, columns = lax.optimization_barrier((arrived, columns))
    rows = exchange_rows(where, *columns)
    parts = add_split((4, 24, PW), 4, parts[0], *arrived)
    arrived = [send(parts[k], along_y(k)) for k in (1, 2, 3)]
    value = add_split((1, 24, PW), 1, parts[0], *arrived)[0]
    value = add_split((1, 24, PW), 1, value, send(value, along_z(1)))[0]
    value, rows = lax.optimization_barrier((value, rows))
    outs = [(2, EXT, PW), (2, PW, TILE_W)]
    obj, middle = vmem_call(object_kernel, "object_update", outs, [], where, obj, *rows, probe)
    object_out = send(middle, from_host())
    value = add_split((1, 24, PW), 1, value, send(value, along_z(2)))[0]
    value = add_split((1, 24, PW), 1, value, send(value, along_z(4)))[0]
    value, object_out = lax.optimization_barrier((value, object_out))
    value = join(value, *[send(value, along_y(k)) for k in (1, 2, 3)])
    value = join(value, *[send(value, along_x(k)) for k in (1, 2, 3)])
    return obj, object_out, value, send(value, core_swap())


def first_windows(current, s, t):
    def packed(half):
        return jnp.concatenate([half[:, : PW // 2], half[:, PW // 2 :]], axis=2)

    def unpacked(value):
        return jnp.concatenate([value[:, :, :HALO], value[:, :, HALO:]], axis=1)

    left = unpacked(send(packed(current[:, :, TILE_W - HALO :]), neighbour(0, 1)))
    right = unpacked(send(packed(current[:, :, :HALO]), neighbour(0, -1)))
    left, right = jnp.where(t == 0, 0.0, left), jnp.where(t == TILES - 1, 0.0, right)
    wide = jnp.concatenate([left, current, right], axis=2)
    top = send(wide[:, PW - HALO :], neighbour(1, 0))
    bottom = send(wide[:, :HALO], neighbour(-1, 0))
    top, bottom = jnp.where(s == 0, 0.0, top), jnp.where(s == STRIPES - 1, 0.0, bottom)
    return jnp.concatenate([top, wide, bottom], axis=1)


def per_device(positions, row_offsets, amplitudes, object_field, probe_field):
    tables = dft_tables()
    stripe, tile = lax.axis_index("stripe"), lax.axis_index("tile")
    core, x, y, z = stripe % 2, (tile % 2) * 2 + (stripe // 2) % 2, tile // 2, stripe // 4
    current = send(object_field, to_host())
    amp = send(amplitudes[0], to_host())
    offset = send(row_offsets, to_host())[0, 2] + HALO
    third = jnp.minimum(offset // 8, 15) * 8
    s, t = z * 4 + x, y * 2 + core
    where = jnp.stack([third, s, t, core, x, y, offset - third]).astype(jnp.int32)

    def outer(unused, state):
        obj, unused, probe, near, far = state
        sums = (near, far)
        gl, gr, obj, probe, _ = run_pass(where, obj, None, probe, sums, amp, tables, False)
        parts = exchange(where, gl, gr)
        gl, gr, obj, probe, rest = run_pass(where, obj, parts, probe, None, amp, tables, True)
        obj, object_out, near, far = exchange_and_total(where, obj, probe, gl, gr, *rest)
        return obj, object_out, probe, near, far

    none = jnp.zeros((16, 24, PW), F32)
    state = (first_windows(current, s, t), current, probe_field, none, none)
    obj, object_out, probe, near, far = lax.fori_loop(0, OUTER, outer, state)
    scratch, args = [pltpu.VMEM((3, PW, PW), F32)], (where, probe, near, far)
    probe_out = vmem_call(probe_kernel, "probe_out", [(2, PW, PW)], scratch, *args, held=False)[0]
    return object_out, probe_out


def solution(mesh):
    placed = (
        P("stripe", "tile"),
        P("stripe", "tile"),
        P("stripe", "tile", None, None),
        P(None, "stripe", "tile"),
        P(),
    )
    return jax.shard_map(
        per_device,
        mesh=mesh,
        in_specs=placed,
        out_specs=(P(None, "stripe", "tile"), P()),
        check_vma=False,
    )
```

```python
import functools
import math

import jax
import jax.numpy as jnp
from jax import lax
from jax.experimental import pallas as pl
from jax.experimental.pallas import tpu as pltpu
from jax.sharding import PartitionSpec as P

PW = 256
HALO = 64
TILE_W = 128
PAT_DEV = 3
OUTER = 2
STRIPES = 32
TILES = 8
EXT = PW + 2 * HALO
LANES = 128
AXES = ("stripe", "tile")
F32 = jnp.float32
BF16 = jnp.bfloat16


def place(x, y, z, core):
    return (z * 4 + (x % 2) * 2 + core) * TILES + y * 2 + x // 2


def physical(flat):
    s, t = flat // TILES, flat % TILES
    return (t % 2) * 2 + (s // 2) % 2, t // 2, s // 4, s % 2


def moved(step):
    pairs = []
    for flat in range(STRIPES * TILES):
        pairs.append((flat, place(*step(*physical(flat)))))
    return pairs


def core_swap():
    return moved(lambda x, y, z, c: (x, y, z, 1 - c))


def along_x(k):
    return moved(lambda x, y, z, c: (x ^ k, y, z, c))


def along_y(k):
    return moved(lambda x, y, z, c: (x, y ^ k, z, c))


def along_z(k):
    return moved(lambda x, y, z, c: (x, y, (z + k) % 8, c))


def next_z():
    return moved(lambda x, y, z, c: (x, y, z ^ 1, c))


def far_z():
    return moved(lambda x, y, z, c: (x, y, (z + (3 if z % 2 else 5)) % 8, c))


def host(s, t):
    return place(s % 4, t // 2, s // 4, t % 2)


def to_host():
    return [(s * TILES + t, host(s, t)) for s in range(STRIPES) for t in range(TILES)]


def from_host():
    return [(there, here) for here, there in to_host()]


def neighbour(ds, dt):
    pairs = []
    for s in range(STRIPES):
        for t in range(TILES):
            pairs.append((host(s, t), host((s + ds) % STRIPES, (t + dt) % TILES)))
    return pairs


def send(value, pairs):
    return lax.ppermute(value, AXES, pairs)


def dft_tables():
    indices = jnp.arange(PW, dtype=jnp.int32)
    phase = indices[:, None] * indices[None, :] % PW
    angles = phase.astype(jnp.float32) * (2.0 * math.pi / PW)
    factor = 1.0 / math.sqrt(PW)
    cosine = (jnp.cos(angles) * factor).astype(jnp.bfloat16)
    sine = (jnp.sin(angles) * factor).astype(jnp.bfloat16)
    forward = jnp.concatenate(
        [jnp.concatenate([cosine, sine], 1), jnp.concatenate([-sine, cosine], 1)], 0
    )
    inverse = jnp.concatenate(
        [jnp.concatenate([cosine, -sine], 1), jnp.concatenate([sine, cosine], 1)], 0
    )
    return forward, inverse


def vmem_call(kernel, name, out_shapes, scratch, *args, held=True, grant=8 << 20):
    smem = pl.BlockSpec(memory_space=pltpu.SMEM)
    vmem = pl.BlockSpec(memory_space=pltpu.VMEM)
    keep = pltpu.with_memory_space_constraint
    args = [a if a.dtype == jnp.int32 else keep(a, pltpu.VMEM) for a in args]
    return pl.pallas_call(
        kernel,
        name=name,
        in_specs=[smem if a.dtype == jnp.int32 else vmem for a in args],
        out_specs=[vmem for _ in out_shapes],
        out_shape=[pltpu.VMEM(s, F32) if held else jax.ShapeDtypeStruct(s, F32) for s in out_shapes],
        scratch_shapes=scratch,
        compiler_params=pltpu.CompilerParams(vmem_limit_bytes=grant),
    )(*args)


def unless(end, value):
    return jnp.where(end, jnp.zeros_like(value), value)


def step_of(probe_ref):
    power = probe_ref[0] * probe_ref[0] + probe_ref[1] * probe_ref[1]
    return 1.0 / (2.0 * PAT_DEV * jnp.max(power) + 1e-06)


def updated(place_ref, probe_ref, obj_ref, parts, store):
    gl, gr, rl, rr, rt, rb = parts
    step = step_of(probe_ref)
    s, t = place_ref[1], place_ref[2]
    row_lo = jnp.where(s == 0, HALO, 0)
    row_hi = jnp.where(s == STRIPES - 1, HALO + PW, EXT)
    col_lo = jnp.where(t == 0, HALO, 0)
    col_hi = jnp.where(t == TILES - 1, HALO + TILE_W, PW)
    for side, own, other, end in ((0, gl, rl, t == 0), (1, gr, rr, t == TILES - 1)):
        cols = slice(side * LANES, (side + 1) * LANES)
        row = lax.broadcasted_iota(jnp.int32, (LANES, LANES), 0)
        col = lax.broadcasted_iota(jnp.int32, (LANES, LANES), 1) + side * LANES
        col_ok = (col >= col_lo) & (col < col_hi)
        for block in range(3):
            span = slice(block * LANES, (block + 1) * LANES)
            at = row + block * LANES
            ok = col_ok & (at >= row_lo) & (at < row_hi)
            factor = jnp.where(ok, step, 0.0)
            for ch in range(2):
                g = own[ch, span, :] + unless(end, other[ch, span, :])
                if block == 0:
                    g = g + unless(s == 0, rt[ch, :, cols])
                if block == 2:
                    g = g + unless(s == STRIPES - 1, rb[ch, :, cols])
                store(ch, block, side, obj_ref[ch, span, cols] - factor * g)


def new_probe(place_ref, probe_ref, near_ref, far_ref, total_ref, out_ref):
    c, x, y = place_ref[3], place_ref[4], place_ref[5]
    for k in range(4):
        for j in range(4):
            block = (x ^ k) * 4 + (y ^ j)
            for half, ref in ((c, near_ref), (1 - c, far_ref)):
                row = pl.multiple_of((half * 16 + block) * 8, 8)
                for ch in range(3):
                    total_ref[ch, pl.ds(row, 8), :] = ref[k * 4 + j, ch * 8 : ch * 8 + 8, :]
    scale = 0.5 / (total_ref[2] + 1.0)
    for ch in range(2):
        out_ref[ch] = probe_ref[ch] - total_ref[ch] * scale


def lifted(value, shift):
    tiles = value.reshape(PW // 8 + 1, 8, value.shape[1])
    tiles = pltpu.roll(tiles, (8 - shift) % 8, axis=1)
    row = lax.broadcasted_iota(jnp.int32, (PW // 8, 8, value.shape[1]), 1)
    return jnp.where(row < 8 - shift, tiles[:-1], tiles[1:]).reshape(PW, value.shape[1])


def lowered(value, shift):
    tiles = value.reshape(PW // 8, 8, value.shape[1])
    tiles = pltpu.roll(tiles, shift % 8, axis=1)
    none = jnp.zeros((1, 8, value.shape[1]), F32)
    row = lax.broadcasted_iota(jnp.int32, (PW // 8 + 1, 8, value.shape[1]), 1)
    below = jnp.concatenate([tiles, none], axis=0)
    above = jnp.concatenate([none, tiles], axis=0)
    return jnp.where(row >= shift, below, above).reshape(PW + 8, value.shape[1])


def patterns(place_ref, obj_ref, probe_ref, amp_ref, fwd_ref, inv_ref, gl_ref, gr_ref, pg_ref):
    fwd, inv = fwd_ref[...], inv_ref[...]
    third, shift = pl.multiple_of(place_ref[0], 8), place_ref[6]
    for p in range(PAT_DEV):
        if p < 2:
            rows = pl.ds((0, 2 * HALO)[p], PW)
            wr, wi = obj_ref[0, rows, :], obj_ref[1, rows, :]
        else:
            wr, wi = [lifted(obj_ref[ch, pl.ds(third, PW + 8), :], shift) for ch in range(2)]
        pr, pi = probe_ref[0], probe_ref[1]
        exit_wave = jnp.concatenate(
            [(pr * wr - pi * wi).astype(BF16), (pr * wi + pi * wr).astype(BF16)], axis=0
        )
        half = jnp.dot(fwd, exit_wave, preferred_element_type=F32)
        half = jnp.concatenate([half[:PW].astype(BF16), half[PW:].astype(BF16)], axis=1)
        spec = jnp.dot(half, inv, preferred_element_type=F32)
        sr, si = spec[:, :PW], spec[:, PW:]
        scaling = amp_ref[p] * lax.rsqrt(jnp.maximum(sr * sr + si * si, 0.25))
        miss = jnp.concatenate(
            [(sr - scaling * sr).astype(BF16), (si - scaling * si).astype(BF16)], axis=0
        )
        half = jnp.dot(inv, miss, preferred_element_type=F32)
        half = jnp.concatenate([half[:PW].astype(BF16), half[PW:].astype(BF16)], axis=1)
        back = jnp.dot(half, fwd, preferred_element_type=F32)
        br, bi = back[:, :PW], back[:, PW:]
        for ch, og in ((0, pr * br + pi * bi), (1, pr * bi - pi * br)):
            for ref, part in ((gl_ref, og[:, :LANES]), (gr_ref, og[:, LANES:])):
                if p == 0:
                    ref[ch, 0:PW, :] = part
                elif p == 1:
                    ref[ch, 2 * HALO : PW, :] += part[: 2 * HALO]
                    ref[ch, PW:EXT, :] = part[2 * HALO :]
                else:
                    ref[ch, pl.ds(third, PW + 8), :] += lowered(part, shift)
        if pg_ref is not None:
            sums = (wr * br + wi * bi, wr * bi - wi * br, wr * wr + wi * wi)
            for ch, value in enumerate(sums):
                if p == 0:
                    pg_ref[ch] = value
                else:
                    pg_ref[ch] += value


def split_probe_grad(place_ref, pg_ref, keep_ref, send_ref):
    c, x, y = place_ref[3], place_ref[4], place_ref[5]
    for k in range(4):
        for j in range(4):
            block = (x ^ k) * 4 + (y ^ j)
            for half, ref in ((c, keep_ref), (1 - c, send_ref)):
                row = pl.multiple_of((half * 16 + block) * 8, 8)
                for ch in range(3):
                    ref[k * 4 + j, ch * 8 : ch * 8 + 8, :] = pg_ref[ch, pl.ds(row, 8), :]


def pass_kernel(first, last_inner, fresh_probe, *refs):
    refs = list(refs)
    place_ref = refs.pop(0)
    obj_ref = refs.pop(0)
    parts = None if first else [refs.pop(0) for _ in range(6)]
    probe_ref = refs.pop(0)
    sums = [refs.pop(0) for _ in range(2)] if fresh_probe else None
    amp_ref, fwd_ref, inv_ref = [refs.pop(0) for _ in range(3)]
    gl_ref, gr_ref = [refs.pop(0) for _ in range(2)]
    if not first:
        out_ref = refs.pop(0)

        def store(ch, block, side, value):
            rows = slice(block * LANES, (block + 1) * LANES)
            out_ref[ch, rows, side * LANES : (side + 1) * LANES] = value

        updated(place_ref, probe_ref, obj_ref, parts, store)
        obj_ref = out_ref
    if fresh_probe:
        fresh_ref = refs.pop(0)
    if last_inner:
        keep_ref, send_ref = [refs.pop(0) for _ in range(2)]
    if fresh_probe:
        new_probe(place_ref, probe_ref, sums[0], sums[1], refs[-1], fresh_ref)
        probe_ref = fresh_ref
    pg_ref = refs[-1] if last_inner else None
    patterns(place_ref, obj_ref, probe_ref, amp_ref, fwd_ref, inv_ref, gl_ref, gr_ref, pg_ref)
    if last_inner:
        split_probe_grad(place_ref, pg_ref, keep_ref, send_ref)


def run_pass(where, obj, parts, probe, sums, amp, tables, last_inner):
    first, fresh = parts is None, sums is not None
    args = [where, obj] + ([] if first else list(parts)) + [probe]
    args += (list(sums) if fresh else []) + [amp, *tables]
    outs = [(2, EXT, LANES)] * 2
    outs += [] if first else [(2, EXT, PW)]
    outs += [(2, PW, PW)] if fresh else []
    outs += [(16, 24, PW)] * 2 if last_inner else []
    scratch = [pltpu.VMEM((3, PW, PW), F32)] if fresh or last_inner else []
    kernel = functools.partial(pass_kernel, first, last_inner, fresh)
    got = list(vmem_call(kernel, "object_pass", outs, scratch, *args, grant=24 << 20))
    gl, gr = got.pop(0), got.pop(0)
    obj = obj if first else got.pop(0)
    probe = got.pop(0) if fresh else probe
    return gl, gr, obj, probe, got


def object_kernel(place_ref, obj_ref, gl, gr, rl, rr, rt, rb, probe_ref, out_ref, middle_ref):
    def store(ch, block, side, value):
        rows = slice(block * LANES, (block + 1) * LANES)
        out_ref[ch, rows, side * LANES : (side + 1) * LANES] = value

    updated(place_ref, probe_ref, obj_ref, (gl, gr, rl, rr, rt, rb), store)
    middle_ref[...] = out_ref[:, HALO : HALO + PW, HALO : HALO + TILE_W]


def probe_kernel(place_ref, probe_ref, near_ref, far_ref, out_ref, total_ref):
    new_probe(place_ref, probe_ref, near_ref, far_ref, total_ref, out_ref)


def exchange_columns(gl, gr):
    return gl, gr, send(gr, neighbour(0, 1)), send(gl, neighbour(0, -1))


def exchange_rows(where, gl, gr, rl, rr):
    def edges(place_ref, gl, gr, rl, rr, top, bottom):
        t = place_ref[2]
        halves = (slice(0, LANES), gl, rl, t == 0), (slice(LANES, PW), gr, rr, t == TILES - 1)
        for ch in range(2):
            for cols, a, b, end in halves:
                top[ch, :, cols] = a[ch, 0:LANES, :] + unless(end, b[ch, 0:LANES, :])
                bottom[ch, :, cols] = a[ch, PW:EXT, :] + unless(end, b[ch, PW:EXT, :])

    top, bottom = vmem_call(edges, "edges", [(2, LANES, PW)] * 2, [], where, gl, gr, rl, rr)
    rt = send(bottom, neighbour(1, 0))
    rb = send(top, neighbour(-1, 0))
    return gl, gr, rl, rr, rt, rb


def add_split(shape, parts, *arrays):
    count = len(arrays)
    rows = shape[0] // parts

    def kernel(*refs):
        ins, outs = refs[:count], refs[count:]
        for k, out in enumerate(outs):
            value = ins[0][k * rows : (k + 1) * rows]
            for ref in ins[1:]:
                value = value + ref[k * rows : (k + 1) * rows]
            out[...] = value

    return vmem_call(kernel, "add_split", [(rows, *shape[1:])] * parts, [], *arrays)


def add_pairs(*arrays):
    def kernel(a, b, c, d, out):
        out[...] = (a[...] + b[...]) + (c[...] + d[...])

    return vmem_call(kernel, "add_pairs", [arrays[0].shape], [], *arrays)[0]


def join(*arrays):
    rows = arrays[0].shape[0]

    def kernel(*refs):
        for k, ref in enumerate(refs[:-1]):
            refs[-1][k * rows : (k + 1) * rows] = ref[...]

    shape = (rows * len(arrays), *arrays[0].shape[1:])
    return vmem_call(kernel, "join", [shape], [], *arrays)[0]


def exchange(where, gl, gr):
    return exchange_rows(where, *exchange_columns(gl, gr))


def exchange_and_total(where, obj, probe, gl, gr, keep, sent):
    columns = exchange_columns(gl, gr)
    arrived = send(sent, core_swap())
    parts = add_split((16, 24, PW), 4, keep, arrived)
    arrived = [send(parts[k], along_x(k)) for k in (1, 2, 3)]
    arrived, columns = lax.optimization_barrier((arrived, columns))
    rows = exchange_rows(where, *columns)
    parts = add_split((4, 24, PW), 4, parts[0], *arrived)
    arrived = [send(parts[k], along_y(k)) for k in (1, 2, 3)]
    value = add_split((1, 24, PW), 1, parts[0], *arrived)[0]
    value = add_split((1, 24, PW), 1, value, send(value, next_z()))[0]
    value, rows = lax.optimization_barrier((value, rows))
    outs = [(2, EXT, PW), (2, PW, TILE_W)]
    obj, middle = vmem_call(object_kernel, "object_update", outs, [], where, obj, *rows, probe)
    object_out = send(middle, from_host())
    value = add_pairs(value, send(value, far_z()), send(value, along_z(2)), send(value, along_z(-2)))
    value, object_out = lax.optimization_barrier((value, object_out))
    value = join(value, *[send(value, along_y(k)) for k in (1, 2, 3)])
    value = join(value, *[send(value, along_x(k)) for k in (1, 2, 3)])
    return obj, object_out, value, send(value, core_swap())


def to_neighbour(dt):
    whole = [(s, t) for s in range(STRIPES) for t in range(TILES) if 0 <= t + dt < TILES]
    return [(s * TILES + t, host(s, t + dt)) for s, t in whole]


def first_windows(own, s, offset):
    def packed(half):
        return jnp.concatenate([half[:, : PW // 2], half[:, PW // 2 :]], axis=2)

    def unpacked(value):
        return jnp.concatenate([value[:, :, :HALO], value[:, :, HALO:]], axis=1)

    tail = jnp.broadcast_to(offset.astype(F32), (2, 8, TILE_W))
    current = send(jnp.concatenate([own, tail], axis=1), to_host())
    left = unpacked(send(packed(own[:, :, TILE_W - HALO :]), to_neighbour(1)))
    right = unpacked(send(packed(own[:, :, :HALO]), to_neighbour(-1)))
    wide = jnp.concatenate([left, current[:, :PW], right], axis=2)
    top = send(wide[:, PW - HALO :], neighbour(1, 0))
    bottom = send(wide[:, :HALO], neighbour(-1, 0))
    top, bottom = jnp.where(s == 0, 0.0, top), jnp.where(s == STRIPES - 1, 0.0, bottom)
    offset = current[0, PW, 0].astype(jnp.int32)
    return jnp.concatenate([top, wide, bottom], axis=1), offset


def per_device(positions, row_offsets, amplitudes, object_field, probe_field):
    tables = dft_tables()
    stripe, tile = lax.axis_index("stripe"), lax.axis_index("tile")
    core, x, y, z = stripe % 2, (tile % 2) * 2 + (stripe // 2) % 2, tile // 2, stripe // 4
    s, t = z * 4 + x, y * 2 + core
    obj, offset = first_windows(object_field, s, row_offsets[0, 2] + HALO)
    amp = send(amplitudes[0], to_host())
    third = jnp.minimum(offset // 8, 15) * 8
    where = jnp.stack([third, s, t, core, x, y, offset - third]).astype(jnp.int32)

    def outer(unused, state):
        obj, unused, probe, near, far = state
        sums = (near, far)
        gl, gr, obj, probe, _ = run_pass(where, obj, None, probe, sums, amp, tables, False)
        parts = exchange(where, gl, gr)
        gl, gr, obj, probe, rest = run_pass(where, obj, parts, probe, None, amp, tables, True)
        obj, object_out, near, far = exchange_and_total(where, obj, probe, gl, gr, *rest)
        return obj, object_out, probe, near, far

    none = jnp.zeros((16, 24, PW), F32)
    state = (obj, object_field, probe_field, none, none)
    obj, object_out, probe, near, far = lax.fori_loop(0, OUTER, outer, state)
    scratch, args = [pltpu.VMEM((3, PW, PW), F32)], (where, probe, near, far)
    probe_out = vmem_call(probe_kernel, "probe_out", [(2, PW, PW)], scratch, *args, held=False)[0]
    return object_out, probe_out


def solution(mesh):
    placed = (
        P("stripe", "tile"),
        P("stripe", "tile"),
        P("stripe", "tile", None, None),
        P(None, "stripe", "tile"),
        P(),
    )
    return jax.shard_map(
        per_device,
        mesh=mesh,
        in_specs=placed,
        out_specs=(P(None, "stripe", "tile"), P()),
        check_vma=False,
    )
```

```python
import functools
import math

import jax
import jax.numpy as jnp
import numpy as np
from jax import lax
from jax.experimental import pallas as pl
from jax.experimental.pallas import tpu as pltpu
from jax.sharding import PartitionSpec as P

PW = 256
HALO = 64
TILE_W = 128
PAT_DEV = 3
OUTER = 2
STRIPES = 32
TILES = 8
EXT = PW + 2 * HALO
LANES = 128
AXES = ("stripe", "tile")
F32 = jnp.float32
BF16 = jnp.bfloat16


def place(x, y, z, core):
    return (z * 4 + (x % 2) * 2 + core) * TILES + y * 2 + x // 2


def physical(flat):
    s, t = flat // TILES, flat % TILES
    return (t % 2) * 2 + (s // 2) % 2, t // 2, s // 4, s % 2


def moved(step):
    pairs = []
    for flat in range(STRIPES * TILES):
        pairs.append((flat, place(*step(*physical(flat)))))
    return pairs


def core_swap():
    return moved(lambda x, y, z, c: (x, y, z, 1 - c))


def along_x(k):
    return moved(lambda x, y, z, c: (x ^ k, y, z, c))


def along_y(k):
    return moved(lambda x, y, z, c: (x, y ^ k, z, c))


def along_z(k):
    return moved(lambda x, y, z, c: (x, y, (z + k) % 8, c))


def next_z():
    return moved(lambda x, y, z, c: (x, y, z ^ 1, c))


def far_z():
    return moved(lambda x, y, z, c: (x, y, (z + (3 if z % 2 else 5)) % 8, c))


def host(s, t):
    return place(s % 4, t // 2, s // 4, t % 2)


def to_host():
    return [(s * TILES + t, host(s, t)) for s in range(STRIPES) for t in range(TILES)]


def from_host():
    return [(there, here) for here, there in to_host()]


def neighbour(ds, dt):
    pairs = []
    for s in range(STRIPES):
        for t in range(TILES):
            pairs.append((host(s, t), host((s + ds) % STRIPES, (t + dt) % TILES)))
    return pairs


def send(value, pairs):
    return lax.ppermute(value, AXES, pairs)


def dft_tables():
    indices = np.arange(PW, dtype=np.int32)
    phase = indices[:, None] * indices[None, :] % PW
    angles = phase.astype(np.float32) * np.float32(2.0 * math.pi / PW)
    factor = np.float32(1.0 / math.sqrt(PW))
    cosine, sine = np.cos(angles) * factor, np.sin(angles) * factor
    forward = np.block([[cosine, sine], [-sine, cosine]]).astype(BF16)
    inverse = np.block([[cosine, -sine], [sine, cosine]]).astype(BF16)
    return jnp.asarray(forward), jnp.asarray(inverse)


def vmem_call(kernel, out_shapes, scratch, *args, held=True, grant=8 << 20):
    smem = pl.BlockSpec(memory_space=pltpu.SMEM)
    vmem = pl.BlockSpec(memory_space=pltpu.VMEM)
    keep = pltpu.with_memory_space_constraint
    args = [a if a.dtype == jnp.int32 else keep(a, pltpu.VMEM) for a in args]
    return pl.pallas_call(
        kernel,
        in_specs=[smem if a.dtype == jnp.int32 else vmem for a in args],
        out_specs=[vmem for _ in out_shapes],
        out_shape=[pltpu.VMEM(s, F32) if held else jax.ShapeDtypeStruct(s, F32) for s in out_shapes],
        scratch_shapes=scratch,
        compiler_params=pltpu.CompilerParams(vmem_limit_bytes=grant),
    )(*args)


def unless(end, value):
    return jnp.where(end, jnp.zeros_like(value), value)


def step_of(probe_ref):
    power = probe_ref[0] * probe_ref[0] + probe_ref[1] * probe_ref[1]
    return 1.0 / (2.0 * PAT_DEV * jnp.max(power) + 1e-06)


def updated(place_ref, probe_ref, obj_ref, parts, store):
    gl, gr, rl, rr, rt, rb = parts
    step = step_of(probe_ref)
    s, t = place_ref[1], place_ref[2]
    row_lo = jnp.where(s == 0, HALO, 0)
    row_hi = jnp.where(s == STRIPES - 1, HALO + PW, EXT)
    col_lo = jnp.where(t == 0, HALO, 0)
    col_hi = jnp.where(t == TILES - 1, HALO + TILE_W, PW)
    for side, own, other, end in ((0, gl, rl, t == 0), (1, gr, rr, t == TILES - 1)):
        cols = slice(side * LANES, (side + 1) * LANES)
        row = lax.broadcasted_iota(jnp.int32, (LANES, LANES), 0)
        col = lax.broadcasted_iota(jnp.int32, (LANES, LANES), 1) + side * LANES
        col_ok = (col >= col_lo) & (col < col_hi)
        for block in range(3):
            span = slice(block * LANES, (block + 1) * LANES)
            at = row + block * LANES
            ok = col_ok & (at >= row_lo) & (at < row_hi)
            factor = jnp.where(ok, step, 0.0)
            for ch in range(2):
                g = own[ch, span, :] + unless(end, other[ch, span, :])
                if block == 0:
                    g = g + unless(s == 0, rt[ch, :, cols])
                if block == 2:
                    g = g + unless(s == STRIPES - 1, rb[ch, :, cols])
                store(ch, block, side, obj_ref[ch, span, cols] - factor * g)


def new_probe(place_ref, probe_ref, near_ref, far_ref, total_ref, out_ref):
    c, x, y = place_ref[3], place_ref[4], place_ref[5]
    for k in range(4):
        for j in range(4):
            block = (x ^ k) * 4 + (y ^ j)
            for half, ref in ((c, near_ref), (1 - c, far_ref)):
                row = pl.multiple_of((half * 16 + block) * 8, 8)
                for ch in range(3):
                    total_ref[ch, pl.ds(row, 8), :] = ref[k * 4 + j, ch * 8 : ch * 8 + 8, :]
    scale = 0.5 / (total_ref[2] + 1.0)
    for ch in range(2):
        out_ref[ch] = probe_ref[ch] - total_ref[ch] * scale


def lifted(value, shift):
    tiles = value.reshape(PW // 8 + 1, 8, value.shape[1])
    tiles = pltpu.roll(tiles, (8 - shift) % 8, axis=1)
    row = lax.broadcasted_iota(jnp.int32, (PW // 8, 8, value.shape[1]), 1)
    return jnp.where(row < 8 - shift, tiles[:-1], tiles[1:]).reshape(PW, value.shape[1])


def lowered(value, shift):
    tiles = value.reshape(PW // 8, 8, value.shape[1])
    tiles = pltpu.roll(tiles, shift % 8, axis=1)
    none = jnp.zeros((1, 8, value.shape[1]), F32)
    row = lax.broadcasted_iota(jnp.int32, (PW // 8 + 1, 8, value.shape[1]), 1)
    below = jnp.concatenate([tiles, none], axis=0)
    above = jnp.concatenate([none, tiles], axis=0)
    return jnp.where(row >= shift, below, above).reshape(PW + 8, value.shape[1])


def patterns(place_ref, obj_ref, probe_ref, amp_ref, fwd_ref, inv_ref, gl_ref, gr_ref, pg_ref):
    fwd, inv = fwd_ref[...], inv_ref[...]
    third, shift = pl.multiple_of(place_ref[0], 8), place_ref[6]
    for p in range(PAT_DEV):
        if p < 2:
            rows = pl.ds((0, 2 * HALO)[p], PW)
            wr, wi = obj_ref[0, rows, :], obj_ref[1, rows, :]
        else:
            wr, wi = [lifted(obj_ref[ch, pl.ds(third, PW + 8), :], shift) for ch in range(2)]
        pr, pi = probe_ref[0], probe_ref[1]
        exit_wave = jnp.concatenate(
            [(pr * wr - pi * wi).astype(BF16), (pr * wi + pi * wr).astype(BF16)], axis=0
        )
        half = jnp.dot(fwd, exit_wave, preferred_element_type=F32)
        half = jnp.concatenate([half[:PW].astype(BF16), half[PW:].astype(BF16)], axis=1)
        spec = jnp.dot(half, inv, preferred_element_type=F32)
        sr, si = spec[:, :PW], spec[:, PW:]
        scaling = amp_ref[p] * lax.rsqrt(jnp.maximum(sr * sr + si * si, 0.25))
        miss = jnp.concatenate(
            [(sr - scaling * sr).astype(BF16), (si - scaling * si).astype(BF16)], axis=0
        )
        half = jnp.dot(inv, miss, preferred_element_type=F32)
        half = jnp.concatenate([half[:PW].astype(BF16), half[PW:].astype(BF16)], axis=1)
        back = jnp.dot(half, fwd, preferred_element_type=F32)
        br, bi = back[:, :PW], back[:, PW:]
        for ch, og in ((0, pr * br + pi * bi), (1, pr * bi - pi * br)):
            for ref, part in ((gl_ref, og[:, :LANES]), (gr_ref, og[:, LANES:])):
                if p == 0:
                    ref[ch, 0:PW, :] = part
                elif p == 1:
                    ref[ch, 2 * HALO : PW, :] += part[: 2 * HALO]
                    ref[ch, PW:EXT, :] = part[2 * HALO :]
                else:
                    ref[ch, pl.ds(third, PW + 8), :] += lowered(part, shift)
        if pg_ref is not None:
            sums = (wr * br + wi * bi, wr * bi - wi * br, wr * wr + wi * wi)
            for ch, value in enumerate(sums):
                if p == 0:
                    pg_ref[ch] = value
                else:
                    pg_ref[ch] += value


def split_probe_grad(place_ref, pg_ref, keep_ref, send_ref):
    c, x, y = place_ref[3], place_ref[4], place_ref[5]
    for k in range(4):
        for j in range(4):
            block = (x ^ k) * 4 + (y ^ j)
            for half, ref in ((c, keep_ref), (1 - c, send_ref)):
                row = pl.multiple_of((half * 16 + block) * 8, 8)
                for ch in range(3):
                    ref[k * 4 + j, ch * 8 : ch * 8 + 8, :] = pg_ref[ch, pl.ds(row, 8), :]


def pass_kernel(first, last_inner, fresh_probe, *refs):
    refs = list(refs)
    place_ref = refs.pop(0)
    obj_ref = refs.pop(0)
    parts = None if first else [refs.pop(0) for _ in range(6)]
    probe_ref = refs.pop(0)
    sums = [refs.pop(0) for _ in range(2)] if fresh_probe else None
    amp_ref, fwd_ref, inv_ref = [refs.pop(0) for _ in range(3)]
    gl_ref, gr_ref = [refs.pop(0) for _ in range(2)]
    if not first:
        out_ref = refs.pop(0)

        def store(ch, block, side, value):
            rows = slice(block * LANES, (block + 1) * LANES)
            out_ref[ch, rows, side * LANES : (side + 1) * LANES] = value

        updated(place_ref, probe_ref, obj_ref, parts, store)
        obj_ref = out_ref
    if fresh_probe:
        fresh_ref = refs.pop(0)
    if last_inner:
        keep_ref, send_ref = [refs.pop(0) for _ in range(2)]
    if fresh_probe:
        new_probe(place_ref, probe_ref, sums[0], sums[1], refs[-1], fresh_ref)
        probe_ref = fresh_ref
    pg_ref = refs[-1] if last_inner else None
    patterns(place_ref, obj_ref, probe_ref, amp_ref, fwd_ref, inv_ref, gl_ref, gr_ref, pg_ref)
    if last_inner:
        split_probe_grad(place_ref, pg_ref, keep_ref, send_ref)


def run_pass(where, obj, parts, probe, sums, amp, tables, last_inner):
    first, fresh = parts is None, sums is not None
    args = [where, obj] + ([] if first else list(parts)) + [probe]
    args += (list(sums) if fresh else []) + [amp, *tables]
    outs = [(2, EXT, LANES)] * 2
    outs += [] if first else [(2, EXT, PW)]
    outs += [(2, PW, PW)] if fresh else []
    outs += [(16, 24, PW)] * 2 if last_inner else []
    scratch = [pltpu.VMEM((3, PW, PW), F32)] if fresh or last_inner else []
    kernel = functools.partial(pass_kernel, first, last_inner, fresh)
    got = list(vmem_call(kernel, outs, scratch, *args, grant=24 << 20))
    gl, gr = got.pop(0), got.pop(0)
    obj = obj if first else got.pop(0)
    probe = got.pop(0) if fresh else probe
    return gl, gr, obj, probe, got


def object_kernel(place_ref, obj_ref, gl, gr, rl, rr, rt, rb, probe_ref, out_ref, middle_ref):
    def store(ch, block, side, value):
        rows = slice(block * LANES, (block + 1) * LANES)
        out_ref[ch, rows, side * LANES : (side + 1) * LANES] = value

    updated(place_ref, probe_ref, obj_ref, (gl, gr, rl, rr, rt, rb), store)
    middle_ref[...] = out_ref[:, HALO : HALO + PW, HALO : HALO + TILE_W]


def probe_kernel(place_ref, probe_ref, near_ref, far_ref, out_ref, total_ref):
    new_probe(place_ref, probe_ref, near_ref, far_ref, total_ref, out_ref)


def exchange_columns(gl, gr):
    return gl, gr, send(gr, neighbour(0, 1)), send(gl, neighbour(0, -1))


def exchange_rows(where, gl, gr, rl, rr):
    def edges(place_ref, gl, gr, rl, rr, top, bottom):
        t = place_ref[2]
        halves = (slice(0, LANES), gl, rl, t == 0), (slice(LANES, PW), gr, rr, t == TILES - 1)
        for ch in range(2):
            for cols, a, b, end in halves:
                top[ch, :, cols] = a[ch, 0:LANES, :] + unless(end, b[ch, 0:LANES, :])
                bottom[ch, :, cols] = a[ch, PW:EXT, :] + unless(end, b[ch, PW:EXT, :])

    shapes = [(2, LANES, PW)] * 2
    top, bottom = vmem_call(edges, shapes, [], where, gl, gr, rl, rr)
    rt = send(bottom, neighbour(1, 0))
    rb = send(top, neighbour(-1, 0))
    return gl, gr, rl, rr, rt, rb


def add_split(shape, parts, *arrays):
    count = len(arrays)
    rows = shape[0] // parts

    def kernel(*refs):
        ins, outs = refs[:count], refs[count:]
        for k, out in enumerate(outs):
            value = ins[0][k * rows : (k + 1) * rows]
            for ref in ins[1:]:
                value = value + ref[k * rows : (k + 1) * rows]
            out[...] = value

    return vmem_call(kernel, [(rows, *shape[1:])] * parts, [], *arrays)


def add_pairs(*arrays):
    def kernel(a, b, c, d, out):
        out[...] = (a[...] + b[...]) + (c[...] + d[...])

    return vmem_call(kernel, [arrays[0].shape], [], *arrays)[0]


def join(*arrays):
    rows = arrays[0].shape[0]

    def kernel(*refs):
        for k, ref in enumerate(refs[:-1]):
            refs[-1][k * rows : (k + 1) * rows] = ref[...]

    shape = (rows * len(arrays), *arrays[0].shape[1:])
    return vmem_call(kernel, [shape], [], *arrays)[0]


def exchange(where, gl, gr):
    return exchange_rows(where, *exchange_columns(gl, gr))


def exchange_and_total(where, obj, probe, gl, gr, keep, sent):
    columns = exchange_columns(gl, gr)
    arrived = send(sent, core_swap())
    parts = add_split((16, 24, PW), 4, keep, arrived)
    arrived = [send(parts[k], along_x(k)) for k in (1, 2, 3)]
    rows = exchange_rows(where, *columns)
    parts = add_split((4, 24, PW), 4, parts[0], *arrived)
    arrived = [send(parts[k], along_y(k)) for k in (1, 2, 3)]
    value = add_split((1, 24, PW), 1, parts[0], *arrived)[0]
    value = add_split((1, 24, PW), 1, value, send(value, next_z()))[0]
    outs = [(2, EXT, PW), (2, PW, TILE_W)]
    obj, middle = vmem_call(object_kernel, outs, [], where, obj, *rows, probe)
    object_out = send(middle, from_host())
    far = send(value, far_z())
    above, below = send(value, along_z(2)), send(value, along_z(-2))
    value = add_pairs(value, far, above, below)
    value, object_out = lax.optimization_barrier((value, object_out))
    value = join(value, *[send(value, along_y(k)) for k in (1, 2, 3)])
    value = join(value, *[send(value, along_x(k)) for k in (1, 2, 3)])
    return obj, object_out, value, send(value, core_swap())


def first_windows(current, s, t):
    def packed(half):
        return jnp.concatenate([half[:, : PW // 2], half[:, PW // 2 :]], axis=2)

    def unpacked(value):
        return jnp.concatenate([value[:, :, :HALO], value[:, :, HALO:]], axis=1)

    left = unpacked(send(packed(current[:, :, TILE_W - HALO :]), neighbour(0, 1)))
    right = unpacked(send(packed(current[:, :, :HALO]), neighbour(0, -1)))
    left, right = jnp.where(t == 0, 0.0, left), jnp.where(t == TILES - 1, 0.0, right)
    wide = jnp.concatenate([left, current, right], axis=2)
    top = send(wide[:, PW - HALO :], neighbour(1, 0))
    bottom = send(wide[:, :HALO], neighbour(-1, 0))
    top, bottom = jnp.where(s == 0, 0.0, top), jnp.where(s == STRIPES - 1, 0.0, bottom)
    return jnp.concatenate([top, wide, bottom], axis=1)


def per_device(positions, row_offsets, amplitudes, object_field, probe_field):
    tables = dft_tables()
    stripe, tile = lax.axis_index("stripe"), lax.axis_index("tile")
    core, x, y, z = stripe % 2, (tile % 2) * 2 + (stripe // 2) % 2, tile // 2, stripe // 4
    s, t = z * 4 + x, y * 2 + core
    current = send(object_field, to_host())
    amp = send(amplitudes[0], to_host())
    offset = send(row_offsets, to_host())[0, 2] + HALO
    obj = first_windows(current, s, t)
    third = jnp.minimum(offset // 8, 15) * 8
    where = jnp.stack([third, s, t, core, x, y, offset - third]).astype(jnp.int32)

    def outer(unused, state):
        obj, unused, probe, near, far = state
        sums = (near, far)
        gl, gr, obj, probe, _ = run_pass(where, obj, None, probe, sums, amp, tables, False)
        parts = exchange(where, gl, gr)
        gl, gr, obj, probe, rest = run_pass(where, obj, parts, probe, None, amp, tables, True)
        obj, object_out, near, far = exchange_and_total(where, obj, probe, gl, gr, *rest)
        return obj, object_out, probe, near, far

    none = jnp.zeros((16, 24, PW), F32)
    state = (obj, jnp.zeros_like(object_field), probe_field, none, none)
    obj, object_out, probe, near, far = lax.fori_loop(0, OUTER, outer, state)
    scratch, args = [pltpu.VMEM((3, PW, PW), F32)], (where, probe, near, far)
    probe_out = vmem_call(probe_kernel, [(2, PW, PW)], scratch, *args, held=False)[0]
    return object_out, probe_out


def solution(mesh):
    placed = (
        P("stripe", "tile"),
        P("stripe", "tile"),
        P("stripe", "tile", None, None),
        P(None, "stripe", "tile"),
        P(),
    )
    return jax.shard_map(
        per_device,
        mesh=mesh,
        in_specs=placed,
        out_specs=(P(None, "stripe", "tile"), P()),
        check_vma=False,
    )
```

```python
import functools
import math

import jax
import jax.numpy as jnp
import numpy as np
from jax import lax
from jax.experimental import pallas as pl
from jax.experimental.pallas import tpu as pltpu
from jax.sharding import PartitionSpec as P

PW = 256
HALO = 64
TILE_W = 128
PAT_DEV = 3
OUTER = 2
STRIPES = 32
TILES = 8
EXT = PW + 2 * HALO
LANES = 128
AXES = ("stripe", "tile")
F32 = jnp.float32
BF16 = jnp.bfloat16


def place(x, y, z, core):
    return (z * 4 + (x % 2) * 2 + core) * TILES + y * 2 + x // 2


def physical(flat):
    s, t = flat // TILES, flat % TILES
    return (t % 2) * 2 + (s // 2) % 2, t // 2, s // 4, s % 2


def moved(step):
    pairs = []
    for flat in range(STRIPES * TILES):
        pairs.append((flat, place(*step(*physical(flat)))))
    return pairs


def core_swap():
    return moved(lambda x, y, z, c: (x, y, z, 1 - c))


def along_x(k):
    return moved(lambda x, y, z, c: (x ^ k, y, z, c))


def along_y(k):
    return moved(lambda x, y, z, c: (x, y ^ k, z, c))


def along_z(k):
    return moved(lambda x, y, z, c: (x, y, (z + k) % 8, c))


def next_z():
    return moved(lambda x, y, z, c: (x, y, z ^ 1, c))


def far_z():
    return moved(lambda x, y, z, c: (x, y, (z + (3 if z % 2 else 5)) % 8, c))


def host(s, t):
    return place(s % 4, t // 2, s // 4, t % 2)


def to_host():
    return [(s * TILES + t, host(s, t)) for s in range(STRIPES) for t in range(TILES)]


def from_host():
    return [(there, here) for here, there in to_host()]


def neighbour(ds, dt):
    pairs = []
    for s in range(STRIPES):
        for t in range(TILES):
            pairs.append((host(s, t), host((s + ds) % STRIPES, (t + dt) % TILES)))
    return pairs


def send(value, pairs):
    return lax.ppermute(value, AXES, pairs)


def dft_tables():
    indices = np.arange(PW, dtype=np.int32)
    phase = indices[:, None] * indices[None, :] % PW
    angles = phase.astype(np.float32) * np.float32(2.0 * math.pi / PW)
    factor = np.float32(1.0 / math.sqrt(PW))
    cosine, sine = np.cos(angles) * factor, np.sin(angles) * factor
    forward = np.block([[cosine, sine], [-sine, cosine]]).astype(BF16)
    inverse = np.block([[cosine, -sine], [sine, cosine]]).astype(BF16)
    return jnp.asarray(forward), jnp.asarray(inverse)


def vmem_call(kernel, out_shapes, scratch, *args, held=True, grant=8 << 20):
    smem = pl.BlockSpec(memory_space=pltpu.SMEM)
    vmem = pl.BlockSpec(memory_space=pltpu.VMEM)
    keep = pltpu.with_memory_space_constraint
    args = [a if a.dtype == jnp.int32 else keep(a, pltpu.VMEM) for a in args]
    return pl.pallas_call(
        kernel,
        in_specs=[smem if a.dtype == jnp.int32 else vmem for a in args],
        out_specs=[vmem for _ in out_shapes],
        out_shape=[pltpu.VMEM(s, F32) if held else jax.ShapeDtypeStruct(s, F32) for s in out_shapes],
        scratch_shapes=scratch,
        compiler_params=pltpu.CompilerParams(vmem_limit_bytes=grant),
    )(*args)


def unless(end, value):
    return jnp.where(end, jnp.zeros_like(value), value)


def step_of(probe_ref):
    power = probe_ref[0] * probe_ref[0] + probe_ref[1] * probe_ref[1]
    return 1.0 / (2.0 * PAT_DEV * jnp.max(power) + 1e-06)


def updated(place_ref, probe_ref, obj_ref, parts, store):
    gl, gr, rl, rr, rt, rb = parts
    step = step_of(probe_ref)
    s, t = place_ref[0], place_ref[1]
    row_lo = jnp.where(s == 0, HALO, 0)
    row_hi = jnp.where(s == STRIPES - 1, HALO + PW, EXT)
    col_lo = jnp.where(t == 0, HALO, 0)
    col_hi = jnp.where(t == TILES - 1, HALO + TILE_W, PW)
    for side, own, other, end in ((0, gl, rl, t == 0), (1, gr, rr, t == TILES - 1)):
        cols = slice(side * LANES, (side + 1) * LANES)
        row = lax.broadcasted_iota(jnp.int32, (LANES, LANES), 0)
        col = lax.broadcasted_iota(jnp.int32, (LANES, LANES), 1) + side * LANES
        col_ok = (col >= col_lo) & (col < col_hi)
        for block in range(3):
            span = slice(block * LANES, (block + 1) * LANES)
            at = row + block * LANES
            ok = col_ok & (at >= row_lo) & (at < row_hi)
            factor = jnp.where(ok, step, 0.0)
            for ch in range(2):
                g = own[ch, span, :] + unless(end, other[ch, span, :])
                if block == 0:
                    g = g + unless(s == 0, rt[ch, :, cols])
                if block == 2:
                    g = g + unless(s == STRIPES - 1, rb[ch, :, cols])
                store(ch, block, side, obj_ref[ch, span, cols] - factor * g)


def new_probe(place_ref, probe_ref, sums, total_ref, out_ref):
    c, x, y = place_ref[2], place_ref[3], place_ref[4]
    for k in range(4):
        for j in range(4):
            block = (x ^ k) * 4 + (y ^ j)
            for half, ref in ((c, sums[k]), (1 - c, sums[4 + k])):
                row = pl.multiple_of((half * 16 + block) * 8, 8)
                for ch in range(3):
                    total_ref[ch, pl.ds(row, 8), :] = ref[j, ch * 8 : ch * 8 + 8, :]
    scale = 0.5 / (total_ref[2] + 1.0)
    for ch in range(2):
        out_ref[ch] = probe_ref[ch] - total_ref[ch] * scale


def lifted(value, shift):
    tiles = value.reshape(PW // 8 + 1, 8, value.shape[1])
    tiles = pltpu.roll(tiles, (8 - shift) % 8, axis=1)
    row = lax.broadcasted_iota(jnp.int32, (PW // 8, 8, value.shape[1]), 1)
    return jnp.where(row < 8 - shift, tiles[:-1], tiles[1:]).reshape(PW, value.shape[1])


def lowered(value, shift):
    tiles = value.reshape(PW // 8, 8, value.shape[1])
    tiles = pltpu.roll(tiles, shift % 8, axis=1)
    none = jnp.zeros((1, 8, value.shape[1]), F32)
    row = lax.broadcasted_iota(jnp.int32, (PW // 8 + 1, 8, value.shape[1]), 1)
    below = jnp.concatenate([tiles, none], axis=0)
    above = jnp.concatenate([none, tiles], axis=0)
    return jnp.where(row >= shift, below, above).reshape(PW + 8, value.shape[1])


def patterns(offset_ref, obj_ref, probe_ref, amp_ref, fwd_ref, inv_ref, gl_ref, gr_ref, pg_ref):
    fwd, inv = fwd_ref[...], inv_ref[...]
    offset = offset_ref[0, 2] + HALO
    third = pl.multiple_of(jnp.minimum(lax.shift_right_logical(offset, 3), 15) * 8, 8)
    shift = offset - third
    for p in range(PAT_DEV):
        if p < 2:
            rows = pl.ds((0, 2 * HALO)[p], PW)
            wr, wi = obj_ref[0, rows, :], obj_ref[1, rows, :]
        else:
            wr, wi = [lifted(obj_ref[ch, pl.ds(third, PW + 8), :], shift) for ch in range(2)]
        pr, pi = probe_ref[0], probe_ref[1]
        exit_wave = jnp.concatenate(
            [(pr * wr - pi * wi).astype(BF16), (pr * wi + pi * wr).astype(BF16)], axis=0
        )
        half = jnp.dot(fwd, exit_wave, preferred_element_type=F32)
        half = jnp.concatenate([half[:PW].astype(BF16), half[PW:].astype(BF16)], axis=1)
        spec = jnp.dot(half, inv, preferred_element_type=F32)
        sr, si = spec[:, :PW], spec[:, PW:]
        scaling = amp_ref[p] * lax.rsqrt(jnp.maximum(sr * sr + si * si, 0.25))
        miss = jnp.concatenate(
            [(sr - scaling * sr).astype(BF16), (si - scaling * si).astype(BF16)], axis=0
        )
        half = jnp.dot(inv, miss, preferred_element_type=F32)
        half = jnp.concatenate([half[:PW].astype(BF16), half[PW:].astype(BF16)], axis=1)
        back = jnp.dot(half, fwd, preferred_element_type=F32)
        br, bi = back[:, :PW], back[:, PW:]
        for ch, og in ((0, pr * br + pi * bi), (1, pr * bi - pi * br)):
            for ref, part in ((gl_ref, og[:, :LANES]), (gr_ref, og[:, LANES:])):
                if p == 0:
                    ref[ch, 0:PW, :] = part
                elif p == 1:
                    ref[ch, 2 * HALO : PW, :] += part[: 2 * HALO]
                    ref[ch, PW:EXT, :] = part[2 * HALO :]
                else:
                    ref[ch, pl.ds(third, PW + 8), :] += lowered(part, shift)
        if pg_ref is not None:
            sums = (wr * br + wi * bi, wr * bi - wi * br, wr * wr + wi * wi)
            for ch, value in enumerate(sums):
                if p == 0:
                    pg_ref[ch] = value
                else:
                    pg_ref[ch] += value


def split_probe_grad(place_ref, pg_ref, keep_ref, send_ref):
    c, x, y = place_ref[2], place_ref[3], place_ref[4]
    for k in range(4):
        for j in range(4):
            block = (x ^ k) * 4 + (y ^ j)
            for half, ref in ((c, keep_ref), (1 - c, send_ref)):
                row = pl.multiple_of((half * 16 + block) * 8, 8)
                for ch in range(3):
                    ref[k * 4 + j, ch * 8 : ch * 8 + 8, :] = pg_ref[ch, pl.ds(row, 8), :]


def pass_kernel(first, last_inner, fresh_probe, *refs):
    refs = list(refs)
    place_ref, offset_ref, obj_ref = [refs.pop(0) for _ in range(3)]
    parts = None if first else [refs.pop(0) for _ in range(6)]
    probe_ref = refs.pop(0)
    sums = [refs.pop(0) for _ in range(8)] if fresh_probe else None
    amp_ref, fwd_ref, inv_ref = [refs.pop(0) for _ in range(3)]
    gl_ref, gr_ref = [refs.pop(0) for _ in range(2)]
    if not first:
        out_ref = refs.pop(0)

        def store(ch, block, side, value):
            rows = slice(block * LANES, (block + 1) * LANES)
            out_ref[ch, rows, side * LANES : (side + 1) * LANES] = value

        updated(place_ref, probe_ref, obj_ref, parts, store)
        obj_ref = out_ref
    if fresh_probe:
        fresh_ref = refs.pop(0)
    if last_inner:
        keep_ref, send_ref = [refs.pop(0) for _ in range(2)]
    if fresh_probe:
        new_probe(place_ref, probe_ref, sums, refs[-1], fresh_ref)
        probe_ref = fresh_ref
    pg_ref = refs[-1] if last_inner else None
    patterns(offset_ref, obj_ref, probe_ref, amp_ref, fwd_ref, inv_ref, gl_ref, gr_ref, pg_ref)
    if last_inner:
        split_probe_grad(place_ref, pg_ref, keep_ref, send_ref)


def run_pass(where, offsets, obj, parts, probe, sums, amp, tables, last_inner):
    first, fresh = parts is None, sums is not None
    args = [where, offsets, obj] + ([] if first else list(parts)) + [probe]
    args += (list(sums) if fresh else []) + [amp, *tables]
    outs = [(2, EXT, LANES)] * 2
    outs += [] if first else [(2, EXT, PW)]
    outs += [(2, PW, PW)] if fresh else []
    outs += [(16, 24, PW)] * 2 if last_inner else []
    scratch = [pltpu.VMEM((3, PW, PW), F32)] if fresh or last_inner else []
    kernel = functools.partial(pass_kernel, first, last_inner, fresh)
    got = list(vmem_call(kernel, outs, scratch, *args, grant=24 << 20))
    gl, gr = got.pop(0), got.pop(0)
    obj = obj if first else got.pop(0)
    probe = got.pop(0) if fresh else probe
    return gl, gr, obj, probe, got


def object_kernel(place_ref, obj_ref, gl, gr, rl, rr, rt, rb, probe_ref, out_ref, middle_ref):
    def store(ch, block, side, value):
        rows = slice(block * LANES, (block + 1) * LANES)
        out_ref[ch, rows, side * LANES : (side + 1) * LANES] = value

    updated(place_ref, probe_ref, obj_ref, (gl, gr, rl, rr, rt, rb), store)
    middle_ref[...] = out_ref[:, HALO : HALO + PW, HALO : HALO + TILE_W]


def last_kernel(place_ref, probe_ref, object_ref, *refs):
    new_probe(place_ref, probe_ref, refs[:8], refs[10], refs[8])
    refs[9][...] = object_ref[...]


def exchange_columns(gl, gr):
    return gl, gr, send(gr, neighbour(0, 1)), send(gl, neighbour(0, -1))


def exchange_rows(where, gl, gr, rl, rr):
    def edges(place_ref, gl, gr, rl, rr, top, bottom):
        t = place_ref[1]
        halves = (slice(0, LANES), gl, rl, t == 0), (slice(LANES, PW), gr, rr, t == TILES - 1)
        for ch in range(2):
            for cols, a, b, end in halves:
                top[ch, :, cols] = a[ch, 0:LANES, :] + unless(end, b[ch, 0:LANES, :])
                bottom[ch, :, cols] = a[ch, PW:EXT, :] + unless(end, b[ch, PW:EXT, :])

    shapes = [(2, LANES, PW)] * 2
    top, bottom = vmem_call(edges, shapes, [], where, gl, gr, rl, rr)
    rt = send(bottom, neighbour(1, 0))
    rb = send(top, neighbour(-1, 0))
    return gl, gr, rl, rr, rt, rb


def add_split(shape, parts, *arrays):
    count = len(arrays)
    rows = shape[0] // parts

    def kernel(*refs):
        ins, outs = refs[:count], refs[count:]
        for k, out in enumerate(outs):
            value = ins[0][k * rows : (k + 1) * rows]
            for ref in ins[1:]:
                value = value + ref[k * rows : (k + 1) * rows]
            out[...] = value

    return vmem_call(kernel, [(rows, *shape[1:])] * parts, [], *arrays)


def add_pairs(*arrays):
    def kernel(a, b, c, d, out):
        out[...] = (a[...] + b[...]) + (c[...] + d[...])

    return vmem_call(kernel, [arrays[0].shape], [], *arrays)[0]


def join(*arrays):
    rows = arrays[0].shape[0]

    def kernel(*refs):
        for k, ref in enumerate(refs[:-1]):
            refs[-1][k * rows : (k + 1) * rows] = ref[...]

    shape = (rows * len(arrays), *arrays[0].shape[1:])
    return vmem_call(kernel, [shape], [], *arrays)[0]


def exchange(where, gl, gr):
    return exchange_rows(where, *exchange_columns(gl, gr))


def exchange_and_total(where, obj, probe, gl, gr, keep, sent):
    columns = exchange_columns(gl, gr)
    arrived = send(sent, core_swap())
    parts = add_split((16, 24, PW), 4, keep, arrived)
    arrived = [send(parts[k], along_x(k)) for k in (1, 2, 3)]
    rows = exchange_rows(where, *columns)
    parts = add_split((4, 24, PW), 4, parts[0], *arrived)
    arrived = [send(parts[k], along_y(k)) for k in (1, 2, 3)]
    value = add_split((1, 24, PW), 1, parts[0], *arrived)[0]
    value = add_split((1, 24, PW), 1, value, send(value, next_z()))[0]
    outs = [(2, EXT, PW), (2, PW, TILE_W)]
    obj, middle = vmem_call(object_kernel, outs, [], where, obj, *rows, probe)
    object_out = send(middle, from_host())
    far = send(value, far_z())
    above, below = send(value, along_z(2)), send(value, along_z(-2))
    value = add_pairs(value, far, above, below)
    value = join(value, *[send(value, along_y(k)) for k in (1, 2, 3)])
    near = [value] + [send(value, along_x(k)) for k in (1, 2, 3)]
    near[3], object_out = lax.optimization_barrier((near[3], object_out))
    return obj, object_out, near + [send(part, core_swap()) for part in near]


def first_windows(current, s, t):
    def packed(half):
        return jnp.concatenate([half[:, : PW // 2], half[:, PW // 2 :]], axis=2)

    def unpacked(value):
        return jnp.concatenate([value[:, :, :HALO], value[:, :, HALO:]], axis=1)

    left = unpacked(send(packed(current[:, :, TILE_W - HALO :]), neighbour(0, 1)))
    right = unpacked(send(packed(current[:, :, :HALO]), neighbour(0, -1)))
    left, right = jnp.where(t == 0, 0.0, left), jnp.where(t == TILES - 1, 0.0, right)
    wide = jnp.concatenate([left, current, right], axis=2)
    top = send(wide[:, PW - HALO :], neighbour(1, 0))
    bottom = send(wide[:, :HALO], neighbour(-1, 0))
    top, bottom = jnp.where(s == 0, 0.0, top), jnp.where(s == STRIPES - 1, 0.0, bottom)
    return jnp.concatenate([top, wide, bottom], axis=1)


def per_device(positions, row_offsets, amplitudes, object_field, probe_field):
    tables = dft_tables()
    stripe, tile = lax.axis_index("stripe"), lax.axis_index("tile")
    core, x, y, z = stripe % 2, (tile % 2) * 2 + (stripe // 2) % 2, tile // 2, stripe // 4
    s, t = z * 4 + x, y * 2 + core
    current = send(object_field, to_host())
    amp = send(amplitudes[0], to_host())
    offsets = send(row_offsets, to_host())
    obj = first_windows(current, s, t)
    where = jnp.stack([s, t, core, x, y]).astype(jnp.int32)

    def outer(unused, state):
        obj, unused, probe, sums = state
        first = run_pass(where, offsets, obj, None, probe, sums, amp, tables, False)
        gl, gr, obj, probe, _ = first
        parts = exchange(where, gl, gr)
        second = run_pass(where, offsets, obj, parts, probe, None, amp, tables, True)
        gl, gr, obj, probe, rest = second
        obj, object_out, sums = exchange_and_total(where, obj, probe, gl, gr, *rest)
        return obj, object_out, probe, sums

    none = [jnp.zeros((4, 24, PW), F32) for _ in range(8)]
    state = (obj, jnp.zeros_like(object_field), probe_field, none)
    obj, object_out, probe, sums = lax.fori_loop(0, OUTER, outer, state)
    scratch, args = [pltpu.VMEM((3, PW, PW), F32)], (where, probe, object_out, *sums)
    outs = [(2, PW, PW), (2, PW, TILE_W)]
    probe_out, object_out = vmem_call(last_kernel, outs, scratch, *args, held=False)
    return object_out, probe_out


def solution(mesh):
    placed = (
        P("stripe", "tile"),
        P("stripe", "tile"),
        P("stripe", "tile", None, None),
        P(None, "stripe", "tile"),
        P(),
    )
    return jax.shard_map(
        per_device,
        mesh=mesh,
        in_specs=placed,
        out_specs=(P(None, "stripe", "tile"), P()),
        check_vma=False,
    )
```

```python
import functools
import math

import jax
import jax.numpy as jnp
import numpy as np
from jax import lax
from jax.experimental import pallas as pl
from jax.experimental.pallas import tpu as pltpu
from jax.sharding import PartitionSpec as P

PW = 256
HALO = 64
TILE_W = 128
PAT_DEV = 3
OUTER = 2
STRIPES = 32
TILES = 8
EXT = PW + 2 * HALO
LANES = 128
AXES = ("stripe", "tile")
F32 = jnp.float32
BF16 = jnp.bfloat16


def place(x, y, z, core):
    return (z * 4 + (x % 2) * 2 + core) * TILES + y * 2 + x // 2


def physical(flat):
    s, t = flat // TILES, flat % TILES
    return (t % 2) * 2 + (s // 2) % 2, t // 2, s // 4, s % 2


def moved(step):
    pairs = []
    for flat in range(STRIPES * TILES):
        pairs.append((flat, place(*step(*physical(flat)))))
    return pairs


def core_swap():
    return moved(lambda x, y, z, c: (x, y, z, 1 - c))


def along_x(k):
    return moved(lambda x, y, z, c: (x ^ k, y, z, c))


def along_y(k):
    return moved(lambda x, y, z, c: (x, y ^ k, z, c))


def along_z(k):
    return moved(lambda x, y, z, c: (x, y, (z + k) % 8, c))


def next_z():
    return moved(lambda x, y, z, c: (x, y, z ^ 1, c))


def far_z():
    return moved(lambda x, y, z, c: (x, y, (z + (3 if z % 2 else 5)) % 8, c))


def host(s, t):
    return place(s % 4, t // 2, s // 4, t % 2)


def to_host():
    return [(s * TILES + t, host(s, t)) for s in range(STRIPES) for t in range(TILES)]


def from_host():
    return [(there, here) for here, there in to_host()]


def neighbour(ds, dt):
    pairs = []
    for s in range(STRIPES):
        for t in range(TILES):
            pairs.append((host(s, t), host((s + ds) % STRIPES, (t + dt) % TILES)))
    return pairs


def send(value, pairs):
    return lax.ppermute(value, AXES, pairs)


def dft_tables():
    indices = np.arange(PW, dtype=np.int32)
    phase = indices[:, None] * indices[None, :] % PW
    angles = phase.astype(np.float32) * np.float32(2.0 * math.pi / PW)
    factor = np.float32(1.0 / math.sqrt(PW))
    cosine, sine = np.cos(angles) * factor, np.sin(angles) * factor
    forward = np.block([[cosine, sine], [-sine, cosine]]).astype(BF16)
    inverse = np.block([[cosine, -sine], [sine, cosine]]).astype(BF16)
    return jnp.asarray(forward), jnp.asarray(inverse)


def vmem_call(kernel, out_shapes, scratch, *args, held=True, grant=8 << 20):
    smem = pl.BlockSpec(memory_space=pltpu.SMEM)
    vmem = pl.BlockSpec(memory_space=pltpu.VMEM)
    keep = pltpu.with_memory_space_constraint
    args = [a if a.dtype == jnp.int32 else keep(a, pltpu.VMEM) for a in args]
    return pl.pallas_call(
        kernel,
        in_specs=[smem if a.dtype == jnp.int32 else vmem for a in args],
        out_specs=[vmem for _ in out_shapes],
        out_shape=[pltpu.VMEM(s, F32) if held else jax.ShapeDtypeStruct(s, F32) for s in out_shapes],
        scratch_shapes=scratch,
        compiler_params=pltpu.CompilerParams(vmem_limit_bytes=grant),
    )(*args)


def unless(end, value):
    return jnp.where(end, jnp.zeros_like(value), value)


def step_of(probe_ref):
    power = probe_ref[0] * probe_ref[0] + probe_ref[1] * probe_ref[1]
    return 1.0 / (2.0 * PAT_DEV * jnp.max(power) + 1e-06)


def updated(place_ref, probe_ref, obj_ref, parts, store):
    gl, gr, rl, rr, rt, rb = parts
    step = step_of(probe_ref)
    s, t = place_ref[0], place_ref[1]
    row_lo = jnp.where(s == 0, HALO, 0)
    row_hi = jnp.where(s == STRIPES - 1, HALO + PW, EXT)
    col_lo = jnp.where(t == 0, HALO, 0)
    col_hi = jnp.where(t == TILES - 1, HALO + TILE_W, PW)
    for side, own, other, end in ((0, gl, rl, t == 0), (1, gr, rr, t == TILES - 1)):
        cols = slice(side * LANES, (side + 1) * LANES)
        row = lax.broadcasted_iota(jnp.int32, (LANES, LANES), 0)
        col = lax.broadcasted_iota(jnp.int32, (LANES, LANES), 1) + side * LANES
        col_ok = (col >= col_lo) & (col < col_hi)
        for block in range(3):
            span = slice(block * LANES, (block + 1) * LANES)
            at = row + block * LANES
            ok = col_ok & (at >= row_lo) & (at < row_hi)
            factor = jnp.where(ok, step, 0.0)
            for ch in range(2):
                g = own[ch, span, :] + unless(end, other[ch, span, :])
                if block == 0:
                    g = g + unless(s == 0, rt[ch, :, cols])
                if block == 2:
                    g = g + unless(s == STRIPES - 1, rb[ch, :, cols])
                store(ch, block, side, obj_ref[ch, span, cols] - factor * g)


def block_row(place_ref, half, k, j):
    x, y = place_ref[3], place_ref[4]
    return pl.multiple_of((half * 16 + (x ^ k) * 4 + (y ^ j)) * 8, 8)


def assemble(place_ref, pieces, out_ref):
    c = place_ref[2]
    for k in range(4):
        for j in range(4):
            for half, ref in ((c, pieces[k]), (1 - c, pieces[4 + k])):
                row = block_row(place_ref, half, k, j)
                for ch in range(2):
                    out_ref[ch, pl.ds(row, 8), :] = ref[j, ch * 8 : ch * 8 + 8, :]


def first_pieces(place_ref, probe_ref, *outs):
    c = place_ref[2]
    for k in range(4):
        for j in range(4):
            for half, ref in ((c, outs[k]), (1 - c, outs[4 + k])):
                row = block_row(place_ref, half, k, j)
                for ch in range(2):
                    ref[j, ch * 8 : ch * 8 + 8, :] = probe_ref[ch, pl.ds(row, 8), :]
    outs[8][...] = jnp.zeros_like(outs[8])


def lifted(value, shift):
    tiles = value.reshape(PW // 8 + 1, 8, value.shape[1])
    tiles = pltpu.roll(tiles, (8 - shift) % 8, axis=1)
    row = lax.broadcasted_iota(jnp.int32, (PW // 8, 8, value.shape[1]), 1)
    return jnp.where(row < 8 - shift, tiles[:-1], tiles[1:]).reshape(PW, value.shape[1])


def lowered(value, shift):
    tiles = value.reshape(PW // 8, 8, value.shape[1])
    tiles = pltpu.roll(tiles, shift % 8, axis=1)
    none = jnp.zeros((1, 8, value.shape[1]), F32)
    row = lax.broadcasted_iota(jnp.int32, (PW // 8 + 1, 8, value.shape[1]), 1)
    below = jnp.concatenate([tiles, none], axis=0)
    above = jnp.concatenate([none, tiles], axis=0)
    return jnp.where(row >= shift, below, above).reshape(PW + 8, value.shape[1])


def patterns(offset_ref, obj_ref, probe_ref, amp_ref, fwd_ref, inv_ref, gl_ref, gr_ref, pg_ref):
    fwd, inv = fwd_ref[...], inv_ref[...]
    offset = offset_ref[0, 2] + HALO
    third = pl.multiple_of(jnp.minimum(lax.shift_right_logical(offset, 3), 15) * 8, 8)
    shift = offset - third
    for p in range(PAT_DEV):
        if p < 2:
            rows = pl.ds((0, 2 * HALO)[p], PW)
            wr, wi = obj_ref[0, rows, :], obj_ref[1, rows, :]
        else:
            wr, wi = [lifted(obj_ref[ch, pl.ds(third, PW + 8), :], shift) for ch in range(2)]
        pr, pi = probe_ref[0], probe_ref[1]
        exit_wave = jnp.concatenate(
            [(pr * wr - pi * wi).astype(BF16), (pr * wi + pi * wr).astype(BF16)], axis=0
        )
        half = jnp.dot(fwd, exit_wave, preferred_element_type=F32)
        half = jnp.concatenate([half[:PW].astype(BF16), half[PW:].astype(BF16)], axis=1)
        spec = jnp.dot(half, inv, preferred_element_type=F32)
        sr, si = spec[:, :PW], spec[:, PW:]
        scaling = amp_ref[p] * lax.rsqrt(jnp.maximum(sr * sr + si * si, 0.25))
        miss = jnp.concatenate(
            [(sr - scaling * sr).astype(BF16), (si - scaling * si).astype(BF16)], axis=0
        )
        half = jnp.dot(inv, miss, preferred_element_type=F32)
        half = jnp.concatenate([half[:PW].astype(BF16), half[PW:].astype(BF16)], axis=1)
        back = jnp.dot(half, fwd, preferred_element_type=F32)
        br, bi = back[:, :PW], back[:, PW:]
        for ch, og in ((0, pr * br + pi * bi), (1, pr * bi - pi * br)):
            for ref, part in ((gl_ref, og[:, :LANES]), (gr_ref, og[:, LANES:])):
                if p == 0:
                    ref[ch, 0:PW, :] = part
                elif p == 1:
                    ref[ch, 2 * HALO : PW, :] += part[: 2 * HALO]
                    ref[ch, PW:EXT, :] = part[2 * HALO :]
                else:
                    ref[ch, pl.ds(third, PW + 8), :] += lowered(part, shift)
        if pg_ref is not None:
            sums = (wr * br + wi * bi, wr * bi - wi * br, wr * wr + wi * wi)
            for ch, value in enumerate(sums):
                if p == 0:
                    pg_ref[ch] = value
                else:
                    pg_ref[ch] += value


def split_probe_grad(place_ref, pg_ref, keep_ref, send_ref):
    c = place_ref[2]
    for k in range(4):
        for j in range(4):
            for half, ref in ((c, keep_ref), (1 - c, send_ref)):
                row = block_row(place_ref, half, k, j)
                for ch in range(3):
                    ref[k * 4 + j, ch * 8 : ch * 8 + 8, :] = pg_ref[ch, pl.ds(row, 8), :]


def pass_kernel(last_inner, *refs):
    refs = list(refs)
    place_ref, offset_ref, obj_ref = [refs.pop(0) for _ in range(3)]
    if last_inner:
        parts = [refs.pop(0) for _ in range(6)]
        probe_ref = refs.pop(0)
    else:
        pieces = [refs.pop(0) for _ in range(8)]
    amp_ref, fwd_ref, inv_ref = [refs.pop(0) for _ in range(3)]
    gl_ref, gr_ref = [refs.pop(0) for _ in range(2)]
    if last_inner:
        out_ref, keep_ref, send_ref, pg_ref = refs

        def store(ch, block, side, value):
            rows = slice(block * LANES, (block + 1) * LANES)
            out_ref[ch, rows, side * LANES : (side + 1) * LANES] = value

        updated(place_ref, probe_ref, obj_ref, parts, store)
        obj_ref = out_ref
    else:
        (probe_ref,), pg_ref = refs, None
        assemble(place_ref, pieces, probe_ref)
    fields = (obj_ref, probe_ref, amp_ref, fwd_ref, inv_ref, gl_ref, gr_ref, pg_ref)
    patterns(offset_ref, *fields)
    if last_inner:
        split_probe_grad(place_ref, pg_ref, keep_ref, send_ref)


def first_pass(where, offsets, obj, pieces, amp, tables):
    outs = [(2, EXT, LANES)] * 2 + [(2, PW, PW)]
    args = (where, offsets, obj, *pieces, amp, *tables)
    kernel = functools.partial(pass_kernel, False)
    return vmem_call(kernel, outs, [], *args, grant=24 << 20)


def second_pass(where, offsets, obj, parts, probe, amp, tables):
    outs = [(2, EXT, LANES)] * 2 + [(2, EXT, PW)] + [(16, 24, PW)] * 2
    args = (where, offsets, obj, *parts, probe, amp, *tables)
    kernel, scratch = functools.partial(pass_kernel, True), [pltpu.VMEM((3, PW, PW), F32)]
    return vmem_call(kernel, outs, scratch, *args, grant=24 << 20)


def object_kernel(place_ref, obj_ref, gl, gr, rl, rr, rt, rb, probe_ref, out_ref, middle_ref):
    def store(ch, block, side, value):
        rows = slice(block * LANES, (block + 1) * LANES)
        out_ref[ch, rows, side * LANES : (side + 1) * LANES] = value

    updated(place_ref, probe_ref, obj_ref, (gl, gr, rl, rr, rt, rb), store)
    middle_ref[...] = out_ref[:, HALO : HALO + PW, HALO : HALO + TILE_W]


def last_kernel(place_ref, *refs):
    assemble(place_ref, refs[:8], refs[8])


def exchange_columns(gl, gr):
    return gl, gr, send(gr, neighbour(0, 1)), send(gl, neighbour(0, -1))


def exchange_rows(where, gl, gr, rl, rr):
    def edges(place_ref, gl, gr, rl, rr, top, bottom):
        t = place_ref[1]
        halves = (slice(0, LANES), gl, rl, t == 0), (slice(LANES, PW), gr, rr, t == TILES - 1)
        for ch in range(2):
            for cols, a, b, end in halves:
                top[ch, :, cols] = a[ch, 0:LANES, :] + unless(end, b[ch, 0:LANES, :])
                bottom[ch, :, cols] = a[ch, PW:EXT, :] + unless(end, b[ch, PW:EXT, :])

    shapes = [(2, LANES, PW)] * 2
    top, bottom = vmem_call(edges, shapes, [], where, gl, gr, rl, rr)
    rt = send(bottom, neighbour(1, 0))
    rb = send(top, neighbour(-1, 0))
    return gl, gr, rl, rr, rt, rb


def add_split(shape, parts, *arrays):
    count = len(arrays)
    rows = shape[0] // parts

    def kernel(*refs):
        ins, outs = refs[:count], refs[count:]
        for k, out in enumerate(outs):
            value = ins[0][k * rows : (k + 1) * rows]
            for ref in ins[1:]:
                value = value + ref[k * rows : (k + 1) * rows]
            out[...] = value

    return vmem_call(kernel, [(rows, *shape[1:])] * parts, [], *arrays)


def new_block(where, probe, *arrays):
    def kernel(place_ref, probe_ref, a, b, c, d, out):
        total = (a[...] + b[...]) + (c[...] + d[...])
        scale = 0.5 / (total[0, 16:24] + 1.0)
        row = block_row(place_ref, place_ref[2], 0, 0)
        for ch in range(2):
            span = slice(ch * 8, ch * 8 + 8)
            out[0, span, :] = probe_ref[ch, pl.ds(row, 8), :] - total[0, span] * scale

    return vmem_call(kernel, [(1, 16, PW)], [], where, probe, *arrays)[0]


def join(*arrays):
    rows = arrays[0].shape[0]

    def kernel(*refs):
        for k, ref in enumerate(refs[:-1]):
            refs[-1][k * rows : (k + 1) * rows] = ref[...]

    shape = (rows * len(arrays), *arrays[0].shape[1:])
    return vmem_call(kernel, [shape], [], *arrays)[0]


def exchange(where, gl, gr):
    return exchange_rows(where, *exchange_columns(gl, gr))


def exchange_and_total(where, obj, probe, gl, gr, keep, sent):
    columns = exchange_columns(gl, gr)
    arrived = send(sent, core_swap())
    parts = add_split((16, 24, PW), 4, keep, arrived)
    arrived = [send(parts[k], along_x(k)) for k in (1, 2, 3)]
    rows = exchange_rows(where, *columns)
    parts = add_split((4, 24, PW), 4, parts[0], *arrived)
    arrived = [send(parts[k], along_y(k)) for k in (1, 2, 3)]
    value = add_split((1, 24, PW), 1, parts[0], *arrived)[0]
    value = add_split((1, 24, PW), 1, value, send(value, next_z()))[0]
    outs = [(2, EXT, PW), (2, PW, TILE_W)]
    obj, middle = vmem_call(object_kernel, outs, [], where, obj, *rows, probe)
    far = send(value, far_z())
    above, below = send(value, along_z(2)), send(value, along_z(-2))
    value = new_block(where, probe, value, far, above, below)
    value = join(value, *[send(value, along_y(k)) for k in (1, 2, 3)])
    near = [value] + [send(value, along_x(k)) for k in (1, 2, 3)]
    return obj, middle, near + [send(part, core_swap()) for part in near]


def first_windows(where, current):
    half, ends = PW // 2, (slice(0, HALO), slice(HALO, TILE_W))

    def pack(cur, to_right, to_left):
        for ch in range(2):
            for k, lanes in enumerate(ends):
                rows = slice(k * half, (k + 1) * half)
                to_right[ch, :, lanes] = cur[ch, rows, ends[1]]
                to_left[ch, :, lanes] = cur[ch, rows, ends[0]]

    def widen(place_ref, cur, from_left, from_right, wide, to_above, to_below):
        t = place_ref[1]
        for ch in range(2):
            wide[ch, :, HALO : HALO + TILE_W] = cur[ch]
            for k, lanes in enumerate(ends):
                rows = slice(k * half, (k + 1) * half)
                wide[ch, rows, 0:HALO] = unless(t == 0, from_left[ch, :, lanes])
                wide[ch, rows, PW - HALO :] = unless(t == TILES - 1, from_right[ch, :, lanes])
            to_above[ch] = wide[ch, 0:HALO]
            to_below[ch] = wide[ch, PW - HALO : PW]

    def stack(place_ref, wide, top, bottom, out):
        s = place_ref[0]
        for ch in range(2):
            out[ch, 0:HALO] = unless(s == 0, top[ch])
            out[ch, HALO : HALO + PW] = wide[ch]
            out[ch, HALO + PW :] = unless(s == STRIPES - 1, bottom[ch])

    to_right, to_left = vmem_call(pack, [(2, half, TILE_W)] * 2, [], current)
    left = send(to_right, neighbour(0, 1))
    right = send(to_left, neighbour(0, -1))
    outs = [(2, PW, PW), (2, HALO, PW), (2, HALO, PW)]
    wide, above, below = vmem_call(widen, outs, [], where, current, left, right)
    top = send(below, neighbour(1, 0))
    bottom = send(above, neighbour(-1, 0))
    return vmem_call(stack, [(2, EXT, PW)], [], where, wide, top, bottom)[0]


def per_device(positions, row_offsets, amplitudes, object_field, probe_field):
    tables = dft_tables()
    stripe, tile = lax.axis_index("stripe"), lax.axis_index("tile")
    core, x, y, z = stripe % 2, (tile % 2) * 2 + (stripe // 2) % 2, tile // 2, stripe // 4
    s, t = z * 4 + x, y * 2 + core
    where = jnp.stack([s, t, core, x, y]).astype(jnp.int32)
    current = send(object_field, to_host())
    amp = send(amplitudes[0], to_host())
    offsets = send(row_offsets, to_host())
    obj = first_windows(where, current)

    def outer(unused, state):
        obj, unused, pieces = state
        gl, gr, probe = first_pass(where, offsets, obj, pieces, amp, tables)
        parts = exchange(where, gl, gr)
        passed = second_pass(where, offsets, obj, parts, probe, amp, tables)
        gl, gr, obj, keep, sent = passed
        return exchange_and_total(where, obj, probe, gl, gr, keep, sent)

    outs = [(4, 16, PW)] * 8 + [(2, PW, TILE_W)]
    *pieces, blank = vmem_call(first_pieces, outs, [], where, probe_field)
    obj, middle, pieces = lax.fori_loop(0, OUTER, outer, (obj, blank, pieces))
    object_out = send(middle, from_host())
    probe_out = vmem_call(last_kernel, [(2, PW, PW)], [], where, *pieces, held=False)[0]
    return object_out, probe_out


def solution(mesh):
    placed = (
        P("stripe", "tile"),
        P("stripe", "tile"),
        P("stripe", "tile", None, None),
        P(None, "stripe", "tile"),
        P(),
    )
    return jax.shard_map(
        per_device,
        mesh=mesh,
        in_specs=placed,
        out_specs=(P(None, "stripe", "tile"), P()),
        check_vma=False,
    )
```

```python
import functools
import math

import jax
import jax.numpy as jnp
import numpy as np
from jax import lax
from jax.experimental import pallas as pl
from jax.experimental.pallas import tpu as pltpu
from jax.sharding import PartitionSpec as P

PW = 256
HALO = 64
TILE_W = 128
PAT_DEV = 3
OUTER = 2
STRIPES = 32
TILES = 8
EXT = PW + 2 * HALO
LANES = 128
AXES = ("stripe", "tile")
F32 = jnp.float32
BF16 = jnp.bfloat16


def place(x, y, z, core):
    return (z * 4 + (x % 2) * 2 + core) * TILES + y * 2 + x // 2


def physical(flat):
    s, t = flat // TILES, flat % TILES
    return (t % 2) * 2 + (s // 2) % 2, t // 2, s // 4, s % 2


def moved(step):
    pairs = []
    for flat in range(STRIPES * TILES):
        pairs.append((flat, place(*step(*physical(flat)))))
    return pairs


def core_swap():
    return moved(lambda x, y, z, c: (x, y, z, 1 - c))


def along_x(k):
    return moved(lambda x, y, z, c: (x ^ k, y, z, c))


def along_y(k):
    return moved(lambda x, y, z, c: (x, y ^ k, z, c))


def along_z(k):
    return moved(lambda x, y, z, c: (x, y, (z + k) % 8, c))


def next_z():
    return moved(lambda x, y, z, c: (x, y, z ^ 1, c))


def far_z():
    return moved(lambda x, y, z, c: (x, y, (z + (3 if z % 2 else 5)) % 8, c))


def host(s, t):
    return place(s % 4, t // 2, s // 4, t % 2)


def to_host():
    return [(s * TILES + t, host(s, t)) for s in range(STRIPES) for t in range(TILES)]


def from_host():
    return [(there, here) for here, there in to_host()]


def neighbour(ds, dt):
    pairs = []
    for s in range(STRIPES):
        for t in range(TILES):
            pairs.append((host(s, t), host((s + ds) % STRIPES, (t + dt) % TILES)))
    return pairs


def send(value, pairs):
    return lax.ppermute(value, AXES, pairs)


def dft_tables():
    indices = np.arange(PW, dtype=np.int32)
    phase = indices[:, None] * indices[None, :] % PW
    angles = phase.astype(np.float32) * np.float32(2.0 * math.pi / PW)
    factor = np.float32(1.0 / math.sqrt(PW))
    cosine, sine = np.cos(angles) * factor, np.sin(angles) * factor
    forward = np.block([[cosine, sine], [-sine, cosine]]).astype(BF16)
    inverse = np.block([[cosine, -sine], [sine, cosine]]).astype(BF16)
    return jnp.asarray(forward), jnp.asarray(inverse)


def vmem_call(kernel, out_shapes, scratch, *args, held=True, grant=8 << 20):
    smem = pl.BlockSpec(memory_space=pltpu.SMEM)
    vmem = pl.BlockSpec(memory_space=pltpu.VMEM)
    keep = pltpu.with_memory_space_constraint
    args = [a if a.dtype == jnp.int32 else keep(a, pltpu.VMEM) for a in args]
    return pl.pallas_call(
        kernel,
        in_specs=[smem if a.dtype == jnp.int32 else vmem for a in args],
        out_specs=[vmem for _ in out_shapes],
        out_shape=[pltpu.VMEM(s, F32) if held else jax.ShapeDtypeStruct(s, F32) for s in out_shapes],
        scratch_shapes=scratch,
        compiler_params=pltpu.CompilerParams(vmem_limit_bytes=grant),
    )(*args)


def unless(end, value):
    return jnp.where(end, jnp.zeros_like(value), value)


def step_of(probe_ref):
    power = probe_ref[0] * probe_ref[0] + probe_ref[1] * probe_ref[1]
    return 1.0 / (2.0 * PAT_DEV * jnp.max(power) + 1e-06)


def updated(place_ref, probe_ref, obj_ref, parts, store):
    gl, gr, rl, rr, rt, rb = parts
    step = step_of(probe_ref)
    s, t = place_ref[0], place_ref[1]
    row_lo = jnp.where(s == 0, HALO, 0)
    row_hi = jnp.where(s == STRIPES - 1, HALO + PW, EXT)
    col_lo = jnp.where(t == 0, HALO, 0)
    col_hi = jnp.where(t == TILES - 1, HALO + TILE_W, PW)
    for side, own, other, end in ((0, gl, rl, t == 0), (1, gr, rr, t == TILES - 1)):
        cols = slice(side * LANES, (side + 1) * LANES)
        row = lax.broadcasted_iota(jnp.int32, (LANES, LANES), 0)
        col = lax.broadcasted_iota(jnp.int32, (LANES, LANES), 1) + side * LANES
        col_ok = (col >= col_lo) & (col < col_hi)
        for block in range(3):
            span = slice(block * LANES, (block + 1) * LANES)
            at = row + block * LANES
            ok = col_ok & (at >= row_lo) & (at < row_hi)
            factor = jnp.where(ok, step, 0.0)
            for ch in range(2):
                g = own[ch, span, :] + unless(end, other[ch, span, :])
                if block == 0:
                    g = g + unless(s == 0, rt[ch, :, cols])
                if block == 2:
                    g = g + unless(s == STRIPES - 1, rb[ch, :, cols])
                store(ch, block, side, obj_ref[ch, span, cols] - factor * g)


def block_row(place_ref, half, k, j):
    x, y = place_ref[3], place_ref[4]
    return pl.multiple_of((half * 16 + (x ^ k) * 4 + (y ^ j)) * 8, 8)


def assemble(place_ref, pieces, out_ref):
    c = place_ref[2]
    for k in range(4):
        for j in range(4):
            for half, ref in ((c, pieces[0]), (1 - c, pieces[1])):
                row = block_row(place_ref, half, k, j)
                for ch in range(2):
                    out_ref[ch, pl.ds(row, 8), :] = ref[k * 4 + j, ch * 8 : ch * 8 + 8, :]


def first_pieces(place_ref, probe_ref, *outs):
    c = place_ref[2]
    for k in range(4):
        for j in range(4):
            for half, ref in ((c, outs[0]), (1 - c, outs[1])):
                row = block_row(place_ref, half, k, j)
                for ch in range(2):
                    ref[k * 4 + j, ch * 8 : ch * 8 + 8, :] = probe_ref[ch, pl.ds(row, 8), :]
    outs[2][...] = jnp.zeros_like(outs[2])


def lifted(value, shift):
    tiles = value.reshape(PW // 8 + 1, 8, value.shape[1])
    tiles = pltpu.roll(tiles, (8 - shift) % 8, axis=1)
    row = lax.broadcasted_iota(jnp.int32, (PW // 8, 8, value.shape[1]), 1)
    return jnp.where(row < 8 - shift, tiles[:-1], tiles[1:]).reshape(PW, value.shape[1])


def lowered(value, shift):
    tiles = value.reshape(PW // 8, 8, value.shape[1])
    tiles = pltpu.roll(tiles, shift % 8, axis=1)
    none = jnp.zeros((1, 8, value.shape[1]), F32)
    row = lax.broadcasted_iota(jnp.int32, (PW // 8 + 1, 8, value.shape[1]), 1)
    below = jnp.concatenate([tiles, none], axis=0)
    above = jnp.concatenate([none, tiles], axis=0)
    return jnp.where(row >= shift, below, above).reshape(PW + 8, value.shape[1])


def patterns(offset_ref, obj_ref, probe_ref, amp_ref, fwd_ref, inv_ref, gl_ref, gr_ref, pg_ref):
    fwd, inv = fwd_ref[...], inv_ref[...]
    offset = offset_ref[0, 2] + HALO
    third = pl.multiple_of(jnp.minimum(lax.shift_right_logical(offset, 3), 15) * 8, 8)
    shift = offset - third
    for p in range(PAT_DEV):
        if p < 2:
            rows = pl.ds((0, 2 * HALO)[p], PW)
            wr, wi = obj_ref[0, rows, :], obj_ref[1, rows, :]
        else:
            wr, wi = [lifted(obj_ref[ch, pl.ds(third, PW + 8), :], shift) for ch in range(2)]
        pr, pi = probe_ref[0], probe_ref[1]
        exit_wave = jnp.concatenate(
            [(pr * wr - pi * wi).astype(BF16), (pr * wi + pi * wr).astype(BF16)], axis=0
        )
        half = jnp.dot(fwd, exit_wave, preferred_element_type=F32)
        half = jnp.concatenate([half[:PW].astype(BF16), half[PW:].astype(BF16)], axis=1)
        spec = jnp.dot(half, inv, preferred_element_type=F32)
        sr, si = spec[:, :PW], spec[:, PW:]
        scaling = amp_ref[p] * lax.rsqrt(jnp.maximum(sr * sr + si * si, 0.25))
        miss = jnp.concatenate(
            [(sr - scaling * sr).astype(BF16), (si - scaling * si).astype(BF16)], axis=0
        )
        half = jnp.dot(inv, miss, preferred_element_type=F32)
        half = jnp.concatenate([half[:PW].astype(BF16), half[PW:].astype(BF16)], axis=1)
        back = jnp.dot(half, fwd, preferred_element_type=F32)
        br, bi = back[:, :PW], back[:, PW:]
        for ch, og in ((0, pr * br + pi * bi), (1, pr * bi - pi * br)):
            for ref, part in ((gl_ref, og[:, :LANES]), (gr_ref, og[:, LANES:])):
                if p == 0:
                    ref[ch, 0:PW, :] = part
                elif p == 1:
                    ref[ch, 2 * HALO : PW, :] += part[: 2 * HALO]
                    ref[ch, PW:EXT, :] = part[2 * HALO :]
                else:
                    ref[ch, pl.ds(third, PW + 8), :] += lowered(part, shift)
        if pg_ref is not None:
            sums = (wr * br + wi * bi, wr * bi - wi * br, wr * wr + wi * wi)
            for ch, value in enumerate(sums):
                if p == 0:
                    pg_ref[ch] = value
                else:
                    pg_ref[ch] += value


def split_probe_grad(place_ref, pg_ref, keep_ref, send_ref):
    c = place_ref[2]
    for k in range(4):
        for j in range(4):
            for half, ref in ((c, keep_ref), (1 - c, send_ref)):
                row = block_row(place_ref, half, k, j)
                for ch in range(3):
                    ref[k * 4 + j, ch * 8 : ch * 8 + 8, :] = pg_ref[ch, pl.ds(row, 8), :]


def pass_kernel(last_inner, *refs):
    refs = list(refs)
    place_ref, offset_ref, obj_ref = [refs.pop(0) for _ in range(3)]
    if last_inner:
        parts = [refs.pop(0) for _ in range(6)]
        probe_ref = refs.pop(0)
    else:
        pieces = [refs.pop(0) for _ in range(2)]
    amp_ref, fwd_ref, inv_ref = [refs.pop(0) for _ in range(3)]
    gl_ref, gr_ref = [refs.pop(0) for _ in range(2)]
    if last_inner:
        out_ref, keep_ref, send_ref, pg_ref = refs

        def store(ch, block, side, value):
            rows = slice(block * LANES, (block + 1) * LANES)
            out_ref[ch, rows, side * LANES : (side + 1) * LANES] = value

        updated(place_ref, probe_ref, obj_ref, parts, store)
        obj_ref = out_ref
    else:
        (probe_ref,), pg_ref = refs, None
        assemble(place_ref, pieces, probe_ref)
    fields = (obj_ref, probe_ref, amp_ref, fwd_ref, inv_ref, gl_ref, gr_ref, pg_ref)
    patterns(offset_ref, *fields)
    if last_inner:
        split_probe_grad(place_ref, pg_ref, keep_ref, send_ref)


def first_pass(where, offsets, obj, pieces, amp, tables):
    outs = [(2, EXT, LANES)] * 2 + [(2, PW, PW)]
    args = (where, offsets, obj, *pieces, amp, *tables)
    kernel = functools.partial(pass_kernel, False)
    return vmem_call(kernel, outs, [], *args, grant=24 << 20)


def second_pass(where, offsets, obj, parts, probe, amp, tables):
    outs = [(2, EXT, LANES)] * 2 + [(2, EXT, PW)] + [(16, 24, PW)] * 2
    args = (where, offsets, obj, *parts, probe, amp, *tables)
    kernel, scratch = functools.partial(pass_kernel, True), [pltpu.VMEM((3, PW, PW), F32)]
    return vmem_call(kernel, outs, scratch, *args, grant=24 << 20)


def object_kernel(place_ref, obj_ref, gl, gr, rl, rr, rt, rb, probe_ref, out_ref, middle_ref):
    def store(ch, block, side, value):
        rows = slice(block * LANES, (block + 1) * LANES)
        out_ref[ch, rows, side * LANES : (side + 1) * LANES] = value

    updated(place_ref, probe_ref, obj_ref, (gl, gr, rl, rr, rt, rb), store)
    middle_ref[...] = out_ref[:, HALO : HALO + PW, HALO : HALO + TILE_W]


def last_kernel(place_ref, near_ref, far_ref, object_ref, probe_out_ref, object_out_ref):
    assemble(place_ref, (near_ref, far_ref), probe_out_ref)
    object_out_ref[...] = object_ref[...]


def exchange_columns(gl, gr):
    return gl, gr, send(gr, neighbour(0, 1)), send(gl, neighbour(0, -1))


def exchange_rows(where, gl, gr, rl, rr):
    def edges(place_ref, gl, gr, rl, rr, top, bottom):
        t = place_ref[1]
        halves = (slice(0, LANES), gl, rl, t == 0), (slice(LANES, PW), gr, rr, t == TILES - 1)
        for ch in range(2):
            for cols, a, b, end in halves:
                top[ch, :, cols] = a[ch, 0:LANES, :] + unless(end, b[ch, 0:LANES, :])
                bottom[ch, :, cols] = a[ch, PW:EXT, :] + unless(end, b[ch, PW:EXT, :])

    shapes = [(2, LANES, PW)] * 2
    top, bottom = vmem_call(edges, shapes, [], where, gl, gr, rl, rr)
    rt = send(bottom, neighbour(1, 0))
    rb = send(top, neighbour(-1, 0))
    return gl, gr, rl, rr, rt, rb


def add_split(shape, parts, *arrays):
    count = len(arrays)
    rows = shape[0] // parts

    def kernel(*refs):
        ins, outs = refs[:count], refs[count:]
        for k, out in enumerate(outs):
            value = ins[0][k * rows : (k + 1) * rows]
            for ref in ins[1:]:
                value = value + ref[k * rows : (k + 1) * rows]
            out[...] = value

    return vmem_call(kernel, [(rows, *shape[1:])] * parts, [], *arrays)


def new_block(where, probe, *arrays):
    def kernel(place_ref, probe_ref, a, b, c, d, out):
        total = (a[...] + b[...]) + (c[...] + d[...])
        scale = 0.5 / (total[0, 16:24] + 1.0)
        row = block_row(place_ref, place_ref[2], 0, 0)
        for ch in range(2):
            span = slice(ch * 8, ch * 8 + 8)
            out[0, span, :] = probe_ref[ch, pl.ds(row, 8), :] - total[0, span] * scale

    return vmem_call(kernel, [(1, 16, PW)], [], where, probe, *arrays)[0]


def join(*arrays):
    rows = arrays[0].shape[0]

    def kernel(*refs):
        for k, ref in enumerate(refs[:-1]):
            refs[-1][k * rows : (k + 1) * rows] = ref[...]

    shape = (rows * len(arrays), *arrays[0].shape[1:])
    return vmem_call(kernel, [shape], [], *arrays)[0]


def exchange(where, gl, gr):
    return exchange_rows(where, *exchange_columns(gl, gr))


def exchange_and_total(where, obj, probe, gl, gr, keep, sent):
    columns = exchange_columns(gl, gr)
    arrived = send(sent, core_swap())
    parts = add_split((16, 24, PW), 4, keep, arrived)
    arrived = [send(parts[k], along_x(k)) for k in (1, 2, 3)]
    rows = exchange_rows(where, *columns)
    parts = add_split((4, 24, PW), 4, parts[0], *arrived)
    arrived = [send(parts[k], along_y(k)) for k in (1, 2, 3)]
    value = add_split((1, 24, PW), 1, parts[0], *arrived)[0]
    value = add_split((1, 24, PW), 1, value, send(value, next_z()))[0]
    outs = [(2, EXT, PW), (2, PW, TILE_W)]
    obj, middle = vmem_call(object_kernel, outs, [], where, obj, *rows, probe)
    object_out = send(middle, from_host())
    far = send(value, far_z())
    above, below = send(value, along_z(2)), send(value, along_z(-2))
    value = new_block(where, probe, value, far, above, below)
    value = join(value, *[send(value, along_y(k)) for k in (1, 2, 3)])
    near = join(value, *[send(value, along_x(k)) for k in (1, 2, 3)])
    near, object_out = lax.optimization_barrier((near, object_out))
    return obj, object_out, near, send(near, core_swap())


def first_windows(where, current):
    half, ends = PW // 2, (slice(0, HALO), slice(HALO, TILE_W))

    def pack(cur, to_right, to_left):
        for ch in range(2):
            for k, lanes in enumerate(ends):
                rows = slice(k * half, (k + 1) * half)
                to_right[ch, :, lanes] = cur[ch, rows, ends[1]]
                to_left[ch, :, lanes] = cur[ch, rows, ends[0]]

    def widen(place_ref, cur, from_left, from_right, wide, to_above, to_below):
        t = place_ref[1]
        for ch in range(2):
            wide[ch, :, HALO : HALO + TILE_W] = cur[ch]
            for k, lanes in enumerate(ends):
                rows = slice(k * half, (k + 1) * half)
                wide[ch, rows, 0:HALO] = unless(t == 0, from_left[ch, :, lanes])
                wide[ch, rows, PW - HALO :] = unless(t == TILES - 1, from_right[ch, :, lanes])
            to_above[ch] = wide[ch, 0:HALO]
            to_below[ch] = wide[ch, PW - HALO : PW]

    def stack(place_ref, wide, top, bottom, out):
        s = place_ref[0]
        for ch in range(2):
            out[ch, 0:HALO] = unless(s == 0, top[ch])
            out[ch, HALO : HALO + PW] = wide[ch]
            out[ch, HALO + PW :] = unless(s == STRIPES - 1, bottom[ch])

    to_right, to_left = vmem_call(pack, [(2, half, TILE_W)] * 2, [], current)
    left = send(to_right, neighbour(0, 1))
    right = send(to_left, neighbour(0, -1))
    outs = [(2, PW, PW), (2, HALO, PW), (2, HALO, PW)]
    wide, above, below = vmem_call(widen, outs, [], where, current, left, right)
    top = send(below, neighbour(1, 0))
    bottom = send(above, neighbour(-1, 0))
    return vmem_call(stack, [(2, EXT, PW)], [], where, wide, top, bottom)[0]


def per_device(positions, row_offsets, amplitudes, object_field, probe_field):
    tables = dft_tables()
    stripe, tile = lax.axis_index("stripe"), lax.axis_index("tile")
    core, x, y, z = stripe % 2, (tile % 2) * 2 + (stripe // 2) % 2, tile // 2, stripe // 4
    s, t = z * 4 + x, y * 2 + core
    where = jnp.stack([s, t, core, x, y]).astype(jnp.int32)
    current = send(object_field, to_host())
    amp = send(amplitudes[0], to_host())
    offsets = send(row_offsets, to_host())
    obj = first_windows(where, current)

    def outer(unused, state):
        obj, unused, *pieces = state
        gl, gr, probe = first_pass(where, offsets, obj, pieces, amp, tables)
        parts = exchange(where, gl, gr)
        passed = second_pass(where, offsets, obj, parts, probe, amp, tables)
        gl, gr, obj, keep, sent = passed
        return exchange_and_total(where, obj, probe, gl, gr, keep, sent)

    outs = [(16, 16, PW)] * 2 + [(2, PW, TILE_W)]
    near, far, blank = vmem_call(first_pieces, outs, [], where, probe_field)
    obj, middle, near, far = lax.fori_loop(0, OUTER, outer, (obj, blank, near, far))
    outs, args = [(2, PW, PW), (2, PW, TILE_W)], (where, near, far, middle)
    probe_out, object_out = vmem_call(last_kernel, outs, [], *args, held=False)
    return object_out, probe_out


def solution(mesh):
    placed = (
        P("stripe", "tile"),
        P("stripe", "tile"),
        P("stripe", "tile", None, None),
        P(None, "stripe", "tile"),
        P(),
    )
    return jax.shard_map(
        per_device,
        mesh=mesh,
        in_specs=placed,
        out_specs=(P(None, "stripe", "tile"), P()),
        check_vma=False,
    )
```
